128 devices in a mesh: dp: 8 (over z, core), expert: 16 (over y, x).
Axes of the slice: x: 4, y: 4, z: 4, core: 2. Of those that a mesh axis runs over, the one named last changes fastest.
Arguments:
- inputs: bfloat16 [16384, 2048], P(('dp', 'expert')), may hold values from -6 to 6
- out_grad: bfloat16 [16384, 2048], P(('dp', 'expert')), may hold values from -6 to 6
- combine: float32 [16384, 8], P(('dp', 'expert')), may hold values from 0 to 1, as said below
- routes: int32 [16384, 8], P(('dp', 'expert')), may hold values from 0 to 63, all different within a row; in each aligned block of 128 rows (0 to 127, 128 to 255, ...) at most 24 rows name the same one
- saved_hidden: bfloat16 [8, 64, 16, 24, 768], P('dp', 'expert'), may hold values from -6 to 6
- down_weight: bfloat16 [64, 2048, 768], P('expert'), may hold values from -0.21875 to 0.21875
- router_weight: bfloat16 [64, 2048], replicated, may hold values from -0.125 to 0.125
Outputs:
- hidden_grad: bfloat16 [8, 64, 16, 24, 768], P('dp', 'expert')
- down_grad: bfloat16 [64, 2048, 768], P('expert', 'dp')
- input_grad: bfloat16 [16384, 2048], P(('dp', 'expert'))
- router_grad: float32 [64, 2048], replicated
The draws below stay inside these ranges and needn't reach their ends.
Inputs may be any that keep to these rules, and one draw needn't show every extreme that they name: `routes`: each token names 8 different experts; among the 128 tokens of one device no expert is named by more than 24 tokens, a bound that some block reaches. `combine`: each token's 8 weights are positive and sum to one.
All inputs are finite; a program needn't handle non-finite values.
Results may differ from the reference program's by a relative error of at most 0.017.
Values may be sent and summed in bfloat16 or wider, within the bound.
A program may use at most 128 MiB of HBM per device.

```python
import math
import jax
import jax.numpy as jnp
import numpy as np
from jax import lax

D = 2048
FF = 768
TOP = 8
TOK_DEV = 128
EXPERTS = 64
CAP = 24
TOKENS = 16384
N_DP = 8
N_EXPERT = 16


def draw_combine(key, part):
    raw_weights = jnp.exp(jax.random.uniform(key, (TOKENS, TOP), jnp.float32, -2.0, 2.0))
    return raw_weights / jnp.sum(raw_weights, axis=1, keepdims=True)


def block_levels(own_key, dims, pieces, low, top_value):
    level = 1.0
    for dim, blocks in pieces:
        steps = jax.random.uniform(jax.random.fold_in(jax.random.fold_in(own_key, 6), dim), (blocks,), jnp.float32, low / len(pieces), top_value / len(pieces))
        level = level * jnp.repeat(jnp.exp(steps), dims[dim] // blocks).reshape((-1,) + (1,) * (len(dims) - 1 - dim))
    return level


def deal_out(stream_key, own, number, rows, number_of, top, reach, slope):
    sequence = jax.random.permutation(stream_key, number_of)
    packed, ordinary = load_shares(number_of, rows * top, reach, slope, True), load_shares(number_of, rows * top, reach, slope, False)
    places = jnp.arange(number_of)

    def named(tallies, offset_by):
        used = int((tallies > 0).sum())
        fixed = max(1, used // 4)
        moved = fixed + (places - fixed + offset_by * (used - fixed)) % max(1, number_of - fixed)
        return jnp.zeros((number_of,), jnp.int32).at[sequence[jnp.where(places < fixed, places, moved)]].set(jnp.asarray(tallies, jnp.int32))

    tallies = jnp.where(number % 4 == 0, named(packed, number // 4), named(ordinary, number - number // 4 - 1))
    mixed = jax.random.permutation(jax.random.fold_in(own, 3), number_of)
    giver, taker = mixed[0:number_of // 2 * 2:2], mixed[1:number_of // 2 * 2:2]
    room = jnp.minimum(tallies[giver] - 1, reach - tallies[taker]) // 2
    room = jnp.where((giver == sequence[0]) | (taker == sequence[0]) | (tallies[taker] == 0), 0, jnp.maximum(room, 0))
    moved = jax.random.randint(jax.random.fold_in(own, 4), (number_of // 2,), 0, 1 << 20) % (room + 1)
    tallies = tallies.at[giver].add(-moved).at[taker].add(moved)
    labels = jnp.searchsorted(jnp.cumsum(tallies), jnp.arange(rows * top), side="right").astype(jnp.int32)
    grid = labels.reshape(top, rows).T
    grid = grid[jax.random.permutation(jax.random.fold_in(own, 1), rows)]
    offset_by = jax.random.randint(jax.random.fold_in(own, 2), (rows, 1), 0, top)
    return jnp.take_along_axis(grid, (jnp.arange(top)[None, :] + offset_by) % top, axis=1)


def load_shares(amount, total, limit, skew, full):
    loads = [(1 << 20) // math.isqrt(rank ** skew) + 1 for rank in range(1, amount + 1)]
    largest = limit if full else min(limit, max(-(-total // amount), total * loads[0] // sum(loads)))
    least = 1 if total - largest >= amount - 1 else 0
    holding, spare = [largest] + [least] * (amount - 1), total - largest - least * (amount - 1)
    while spare > 0:
        free = [i for i in range(1, amount) if holding[i] < largest] or [i for i in range(1, amount) if holding[i] < limit]
        mass, left = sum([loads[i] for i in free]), spare
        for i in free:
            addition = min(limit - holding[i], max(1, left * loads[i] // mass), spare)
            holding[i] = holding[i] + addition
            spare = spare - addition
    return np.array(holding)


def gaussian(rng, shape, spread, most, split=(), held_as=jnp.bfloat16):
    level = block_levels(rng, shape, split, -0.22, 0.18) if split else 1.0
    result = jax.random.normal(rng, shape, jnp.float32) * spread * level
    return jnp.minimum(jnp.maximum(result, -most), most).astype(held_as)


def setup_inputs(seed: int = 0) -> dict:
    keys = jax.random.split(jax.random.key(seed), 8)
    inputs = gaussian(keys[0], (TOKENS, D), 1.0, 6.0, ((0, 128),))
    out_grad = gaussian(keys[1], (TOKENS, D), 1.0, 6.0, ((0, 128),))
    combine = draw_combine(jax.random.fold_in(keys[7], 71), 0)
    routes_keys = jax.random.split(jax.random.fold_in(keys[3], 1), TOKENS // TOK_DEV)
    routes_turns = jax.random.permutation(jax.random.fold_in(keys[3], 3), TOKENS // TOK_DEV)
    routes = jax.vmap(lambda own, number: deal_out(jax.random.fold_in(keys[3], 2), own, number, TOK_DEV, EXPERTS, TOP, CAP, 2))(routes_keys, routes_turns).reshape((TOKENS, TOP))
    saved_hidden = gaussian(keys[4], (N_DP, EXPERTS, N_EXPERT, CAP, FF), 1.0, 6.0, ((0, 8), (1, 16)))
    down_weight = gaussian(keys[5], (EXPERTS, D, FF), FF ** -0.5, 0.21875, ((0, 16),))
    router_weight = gaussian(keys[6], (EXPERTS, D), D ** -0.5, 0.125)
    return {"inputs": inputs, "out_grad": out_grad, "combine": combine, "routes": routes, "saved_hidden": saved_hidden, "down_weight": down_weight, "router_weight": router_weight}


def slot_positions(block_routes):
    marks = (block_routes[:, :, None] == jnp.arange(EXPERTS, dtype=jnp.int32)[None, None, :]).astype(jnp.int32)
    counts = jnp.sum(marks, axis=1)
    before = jnp.cumsum(counts, axis=0) - counts
    return jnp.sum(marks * before[:, None, :], axis=2).astype(jnp.int32)


def reference(inputs, out_grad, combine, routes, saved_hidden, down_weight, router_weight):
    blocks = routes.reshape(N_DP * N_EXPERT, TOK_DEV, TOP)
    positions = jax.vmap(slot_positions)(blocks).reshape(TOKENS, TOP)
    token_ids = jnp.arange(TOKENS, dtype=jnp.int32)
    device = token_ids // TOK_DEV
    group_ids = device // N_EXPERT
    source = device % N_EXPERT
    slot_flat = ((group_ids[:, None] * EXPERTS + routes) * N_EXPERT + source[:, None]) * CAP + positions
    slot_total = N_DP * EXPERTS * N_EXPERT * CAP
    pair_total = TOKENS * TOP
    owner_pair = jnp.full((slot_total,), pair_total, jnp.int32)
    owner_pair = owner_pair.at[slot_flat.reshape(-1)].set(jnp.arange(pair_total, dtype=jnp.int32))
    owner_pair = owner_pair.reshape(N_DP, EXPERTS, N_EXPERT * CAP)
    flat_combine = combine.reshape(-1)

    def one_expert(expert):
        pair_ids = lax.dynamic_index_in_dim(owner_pair, expert, 1, keepdims=False)
        filled = pair_ids < pair_total
        safe_pair = jnp.where(filled, pair_ids, 0)
        gain_values = jnp.where(filled, flat_combine[safe_pair], jnp.zeros((), jnp.float32))
        slot_rows = (gain_values[:, :, None] * out_grad[safe_pair // TOP].astype(jnp.float32)).astype(jnp.bfloat16)
        slot_acts = lax.dynamic_index_in_dim(saved_hidden, expert, 1, keepdims=False).reshape(N_DP, N_EXPERT * CAP, FF)
        weight = lax.dynamic_index_in_dim(down_weight, expert, 0, keepdims=False)
        flat_rows = slot_rows.reshape(-1, D)
        flat_hidden = slot_acts.reshape(-1, FF)
        recomputed = lax.dot_general(flat_hidden, weight, (((1,), (1,)), ((), ())), preferred_element_type=jnp.float32)
        products = jnp.sum(recomputed * flat_rows.astype(jnp.float32), axis=1)
        hidden_part = jnp.dot(flat_rows, weight, preferred_element_type=jnp.float32).astype(jnp.bfloat16)
        partial_grads = jnp.einsum('gsd,gsf->gdf', slot_rows.astype(jnp.float32), slot_acts.astype(jnp.float32))
        rounded = lax.optimization_barrier(partial_grads.astype(jnp.bfloat16))
        weight_part = jnp.sum(rounded.astype(jnp.float32), axis=0).astype(jnp.bfloat16)
        return products, hidden_part, weight_part

    products, hidden_parts, down_grad = lax.map(one_expert, jnp.arange(EXPERTS, dtype=jnp.int32))
    hidden_grad = hidden_parts.reshape(EXPERTS, N_DP, N_EXPERT, CAP, FF).transpose(1, 0, 2, 3, 4)
    product_flat = products.reshape(EXPERTS, N_DP, N_EXPERT, CAP).transpose(1, 0, 2, 3).reshape(-1)
    pair_sums = product_flat[slot_flat]
    logit_grad = pair_sums - combine * jnp.sum(pair_sums, axis=1, keepdims=True)
    route_marks = routes[:, :, None] == jnp.arange(EXPERTS, dtype=jnp.int32)[None, None, :]
    dense_grad = jnp.sum(jnp.where(route_marks, logit_grad[:, :, None], jnp.zeros((), jnp.float32)), axis=1).astype(jnp.bfloat16)
    input_grad = jnp.dot(dense_grad, router_weight, preferred_element_type=jnp.float32).astype(jnp.bfloat16)
    router_grad = lax.dot_general(dense_grad, inputs, (((0,), (0,)), ((), ())), preferred_element_type=jnp.float32)
    return hidden_grad, down_grad, input_grad, router_grad
```

```python
import jax
import jax.numpy as jnp
from jax import lax
from jax.experimental import pallas as pl
from jax.experimental.pallas import tpu as pltpu
from jax.sharding import PartitionSpec as P

NX = 4
NY = 4
NZ = 4
NE = NX * NY
NDP = 2 * NZ
TICKS = 8
LANE = 128
BF = jnp.bfloat16
F32 = jnp.float32


def remote(src, dst, ssem, rsem, dev):
    return pltpu.make_async_remote_copy(
        src_ref=src, dst_ref=dst, send_sem=ssem, recv_sem=rsem,
        device_id=dev, device_id_type=pl.DeviceIdType.MESH,
    )


def fused(
    meta_hbm, og_hbm, hid_hbm, w_hbm, in_hbm, rw_hbm,
    hg_out, dw_out, ig_out, rp_out,
    G, W, H, HG, HGB, X, S, GAIN, META, CODES, GROW, DWS, RR, RSEND, RRECV,
    INP, RW, IG, RP,
    ag_s, ag_r, own_s, w_s, misc_s, dws_s, hgb_s, out_s, meta_s, meta_r, ret_s, ret_r,
):
    n_exp, slots, width_ff = hid_hbm.shape
    cap = slots // NE
    pair = 2 * cap
    me = lax.axis_index("expert")
    dp = lax.axis_index("dp")
    y, x = me // NX, lax.rem(me, NX)
    z, c = dp // 2, lax.rem(dp, 2)

    def expert_dev(index):
        return {"expert": index}

    def column(t, h):
        u = t // 2
        step = jnp.where(u == 0, 2, jnp.where(u == 1, 1, jnp.where(u == 2, 3, 0)))
        zz = lax.rem(z + step, NZ)
        core = 1 - c if h == 0 else c
        return pl.multiple_of((2 * zz + core) * 256 + lax.rem(t, 2) * LANE, LANE)

    def axes(h):
        return (x, y) if h == 0 else (y, x)

    def cell(t, h, a, b):
        return G.at[t, h, b, a] if h == 0 else G.at[t, h, a, b]

    def dev(h, a, b):
        return expert_dev(b * NX + a) if h == 0 else expert_dev(a * NX + b)

    def line(t, h, b, lo, n):
        return G.at[t, h, b, pl.ds(lo, n)] if h == 0 else G.at[t, h, pl.ds(lo, n), b]

    def up(i):
        return lax.rem(i + 1, 4)

    def down(i):
        return lax.rem(i + 3, 4)

    def far(i):
        return lax.rem(i + 2, 4)

    def hop(t, h, k):
        a, b = axes(h)
        if k == 0:
            return cell(t, h, a, b), cell(t, h, down(a), b), dev(h, up(a), b)
        if k == 1:
            return cell(t, h, a, b), cell(t, h, up(a), b), dev(h, down(a), b)
        if k == 2:
            lo = pl.ds(0, 64)
            return cell(t, h, down(a), b).at[lo], cell(t, h, far(a), b).at[lo], dev(h, up(a), b)
        if k == 3:
            hi = pl.ds(64, 64)
            return cell(t, h, up(a), b).at[hi], cell(t, h, far(a), b).at[hi], dev(h, down(a), b)
        if k == 4:
            return line(t, h, b, 0, 4), line(t, h, down(b), 0, 4), dev(h, a, up(b))
        if k == 5:
            return line(t, h, b, 0, 4), line(t, h, up(b), 0, 4), dev(h, a, down(b))
        if k == 6:
            return line(t, h, down(b), 0, 2), line(t, h, far(b), 0, 2), dev(h, a, up(b))
        return line(t, h, up(b), 2, 2), line(t, h, far(b), 2, 2), dev(h, a, down(b))

    def hop_start(t, h, k):
        sent, _, to = hop(t, h, k)
        remote(sent, sent, ag_s.at[t, h, k], ag_r.at[t, h, k], to).start()

    def hop_wait(t, h, k):
        _, got, to = hop(t, h, k)
        remote(got, got, ag_s.at[t, h, k], ag_r.at[t, h, k], to).wait_recv()

    def hop_drain(t, h, k):
        sent, _, to = hop(t, h, k)
        remote(sent, sent, ag_s.at[t, h, k], ag_r.at[t, h, k], to).wait_send()

    def own_copy(t, h):
        a, b = axes(h)
        return pltpu.make_async_copy(
            og_hbm.at[:, pl.ds(column(t, h), LANE)], cell(t, h, a, b), own_s.at[t, h]
        )

    def w_copy(t, h):
        return pltpu.make_async_copy(
            w_hbm.at[:, pl.ds(column(t, h), LANE), :], W.at[t, :, h], w_s.at[t, h]
        )

    def dw_copy(t, h):
        return pltpu.make_async_copy(
            DWS.at[lax.rem(t, 2), h], dw_out.at[:, pl.ds(column(t, h), LANE), :],
            dws_s.at[lax.rem(t, 2), h],
        )

    meta_own = pltpu.make_async_copy(meta_hbm, META.at[me], misc_s.at[0])
    meta_own.start()
    for t in range(TICKS):
        for h in range(2):
            own_copy(t, h).start()
    hid_copy = pltpu.make_async_copy(hid_hbm, H, misc_s.at[1])
    in_copy = pltpu.make_async_copy(in_hbm, INP, misc_s.at[2])
    rw_copy = pltpu.make_async_copy(rw_hbm, RW, misc_s.at[3])

    barrier = pltpu.get_barrier_semaphore()
    for d in range(1, NE):
        pl.semaphore_signal(barrier, inc=1, device_id=expert_dev(lax.rem(me + d, NE)),
                            device_id_type=pl.DeviceIdType.MESH)
    hid_copy.start()
    for t in range(TICKS):
        for h in range(2):
            w_copy(t, h).start()
    in_copy.start()
    rw_copy.start()
    pl.semaphore_wait(barrier, NE - 1)

    meta_own.wait()

    def plane_to(d):
        return expert_dev(lax.rem(me + d, NE))

    def plane_from(d):
        return lax.rem(me + NE - d, NE)

    def meta_send(d):
        return remote(META.at[me], META.at[me], meta_s.at[d], meta_r.at[d], plane_to(d))

    def meta_recv(d):
        got = META.at[plane_from(d)]
        return remote(got, got, meta_s.at[d], meta_r.at[d], plane_to(d))

    def build_dispatch():
        for d in range(1, NE):
            meta_recv(d).wait_recv()

        @pl.loop(0, NE // 2)
        def _(p):
            marks, gains = [], []
            for s2 in range(2):
                block = META[2 * p + s2]
                cb, rt = block[0:8], block[8:16]
                for e in range(n_exp):
                    hit = rt == (me * n_exp + e).astype(F32)
                    marks.append(jnp.sum(jnp.where(hit, 1.0, 0.0), axis=0, keepdims=True))
                    gains.append(jnp.sum(jnp.where(hit, cb, 0.0), axis=0, keepdims=True))
            at = pl.multiple_of(p * 8, 8)
            CODES[pl.ds(at, 8), :] = jnp.concatenate(marks, axis=0)
            GROW[pl.ds(at, 8), :] = jnp.concatenate(gains, axis=0)

        marks = CODES[...]
        r = lax.broadcasted_iota(jnp.int32, (LANE, LANE), 0)
        q = lax.broadcasted_iota(jnp.int32, (LANE, LANE), 1)
        earlier = jnp.where(r < q, 1.0, 0.0).astype(BF)
        before = jnp.dot(marks.astype(BF), earlier, preferred_element_type=F32)
        CODES[...] = jnp.where(marks > 0.5, before, -1000.0)

        @pl.loop(0, NE // 2)
        def _(p):
            at = pl.multiple_of(p * 8, 8)
            codes = CODES[pl.ds(at, 8), :]
            gains = GROW[pl.ds(at, 8), :]
            place = lax.broadcasted_iota(jnp.int32, (pair, LANE), 0).astype(F32)
            for e in range(n_exp):
                first = jnp.where(place == codes[e:e + 1], 1.0, 0.0)
                second = jnp.where(place - cap == codes[n_exp + e:n_exp + e + 1], 1.0, 0.0)
                S[p, e * pair:(e + 1) * pair, 0:LANE] = first.astype(BF)
                S[p, e * pair:(e + 1) * pair, LANE:2 * LANE] = second.astype(BF)
                gain = jnp.sum(
                    first * gains[e:e + 1] + second * gains[n_exp + e:n_exp + e + 1],
                    axis=1, keepdims=True,
                )
                GAIN[p, e * pair:(e + 1) * pair, :] = jnp.broadcast_to(gain, (pair, LANE))

    def compute(t):
        for h in range(2):
            w_copy(t, h).wait()
        for p in range(NE // 2):
            yy, xx = p // 2, 2 * (p % 2)
            g0 = G[t, 0, yy, xx:xx + 2].reshape(2 * LANE, LANE)
            g1 = G[t, 1, yy, xx:xx + 2].reshape(2 * LANE, LANE)
            rows = jnp.dot(S[p], jnp.concatenate([g0, g1], axis=1), preferred_element_type=F32)
            gain = GAIN[p]
            rows = (rows * jnp.concatenate([gain, gain], axis=1)).astype(BF)
            for e in range(n_exp):
                X[e, p * pair:(p + 1) * pair, :] = rows[e * pair:(e + 1) * pair]

        @pl.when(t >= 2)
        def _():
            for h in range(2):
                dw_copy(t - 2, h).wait()

        @pl.loop(0, n_exp)
        def _(e):
            xe = X[e]
            we = W[t, e].reshape(2 * LANE, width_ff)
            HG[e] += jnp.dot(xe, we, preferred_element_type=F32)
            grad = lax.dot_general(xe, H[e], (((0,), (0,)), ((), ())), preferred_element_type=F32)
            DWS[lax.rem(t, 2), 0, e] = grad[:LANE].astype(BF)
            DWS[lax.rem(t, 2), 1, e] = grad[LANE:].astype(BF)

        for h in range(2):
            dw_copy(t, h).start()

    @pl.loop(0, TICKS + 4)
    def _(i):
        @pl.when(i < TICKS)
        def _():
            for h in range(2):
                own_copy(i, h).wait()
                hop_start(i, h, 0)
                hop_start(i, h, 1)

        @pl.when(i == 0)
        def _():
            for d in range(1, NE):
                meta_send(d).start()
            hid_copy.wait()
            HG[...] = jnp.zeros_like(HG)

        for phase in range(3):
            @pl.when((i > phase) & (i <= TICKS + phase))
            def _(phase=phase):
                t = i - 1 - phase
                for h in range(2):
                    for k in (2 * phase, 2 * phase + 1):
                        hop_wait(t, h, k)
                        if phase != 1:
                            hop_start(t, h, k + 2)
                if phase == 1:
                    for h in range(2):
                        hop_start(t, h, 4)
                        hop_start(t, h, 5)

        @pl.when(i == 3)
        def _():
            build_dispatch()

        @pl.when(i >= 4)
        def _():
            t = i - 4
            for h in range(2):
                hop_wait(t, h, 6)
                hop_wait(t, h, 7)
            compute(t)

    for e in range(n_exp):
        hg = HG[e]
        HGB[e] = hg.astype(BF)
        pltpu.make_async_copy(HGB.at[e], hg_out.at[e], hgb_s.at[e]).start()
        prod = jnp.sum(H[e].astype(F32) * hg, axis=1, keepdims=True)
        for p in range(NE // 2):
            row = jnp.sum(
                S[p, e * pair:(e + 1) * pair, :].astype(F32) * prod[p * pair:(p + 1) * pair],
                axis=0, keepdims=True,
            )
            RR[p, e:e + 1, :] = row
            RR[p, n_exp + e:n_exp + e + 1, :] = row
    half = lax.broadcasted_iota(jnp.int32, (8, LANE), 0) // n_exp
    mine = half == lax.rem(me, 2)
    for p in range(NE // 2):
        for s2 in range(2):
            RSEND[2 * p + s2] = jnp.where(mine, RR[p, :, s2 * LANE:(s2 + 1) * LANE], 0.0)

    def ret_send(d):
        out = RSEND.at[lax.rem(me + d, NE)]
        return remote(out, RRECV.at[me], ret_s.at[d], ret_r.at[d], plane_to(d))

    def ret_recv(d):
        got = RRECV.at[plane_from(d)]
        return remote(got, got, ret_s.at[d], ret_r.at[d], plane_to(d))

    for d in range(1, NE):
        ret_send(d).start()
    RRECV[me] = RSEND[me]

    own_meta = META[me]
    expert_id = lax.broadcasted_iota(jnp.int32, (NE * n_exp, LANE), 0).astype(F32)
    gate = jnp.zeros((NE * n_exp, LANE), F32)
    named = jnp.zeros((NE * n_exp, LANE), F32)
    for k in range(8):
        hit = expert_id == own_meta[8 + k:9 + k]
        gate += jnp.where(hit, own_meta[k:k + 1], 0.0)
        named += jnp.where(hit, 1.0, 0.0)

    in_copy.wait()
    rw_copy.wait()
    for d in range(1, NE):
        ret_recv(d).wait_recv()
    sums = jnp.concatenate([RRECV[2 * q] + RRECV[2 * q + 1] for q in range(NE // 2)], axis=0)
    total = jnp.sum(sums, axis=0, keepdims=True)
    dense = jnp.where(named > 0.5, sums - gate * total, 0.0).astype(BF)
    for q in range(4):
        cols = slice(q * 512, (q + 1) * 512)
        IG[:, cols] = lax.dot_general(
            dense, RW[:, cols], (((0,), (0,)), ((), ())), preferred_element_type=F32
        ).astype(BF)
        RP[:, cols] = jnp.dot(dense, INP[:, cols], preferred_element_type=F32)
    ig_copy = pltpu.make_async_copy(IG, ig_out, out_s.at[0])
    rp_copy = pltpu.make_async_copy(RP, rp_out, out_s.at[1])
    ig_copy.start()
    rp_copy.start()

    @pl.loop(0, TICKS)
    def _(t):
        for h in range(2):
            for k in range(8):
                hop_drain(t, h, k)

    for d in range(1, NE):
        meta_send(d).wait_send()
        ret_send(d).wait_send()
    for t in (TICKS - 2, TICKS - 1):
        for h in range(2):
            dw_copy(t, h).wait()
    for e in range(n_exp):
        pltpu.make_async_copy(HGB.at[e], hg_out.at[e], hgb_s.at[e]).wait()
    ig_copy.wait()
    rp_copy.wait()


def local(inputs, out_grad, combine, routes, saved_hidden, down_weight, router_weight):
    tokens, width = out_grad.shape
    n_exp, _, ff = down_weight.shape
    total = router_weight.shape[0]
    slots = saved_hidden.shape[2] * saved_hidden.shape[3]
    pair = slots // (NE // 2)
    meta = jnp.concatenate([combine.T, routes.T.astype(F32)], axis=0)
    hidden = saved_hidden.reshape(n_exp, slots, ff)
    dma = pltpu.SemaphoreType.DMA
    hg, dw, ig, rp = pl.pallas_call(
        fused,
        out_shape=(
            jax.ShapeDtypeStruct((n_exp, slots, ff), BF),
            jax.ShapeDtypeStruct((n_exp, width, ff), BF),
            jax.ShapeDtypeStruct((tokens, width), BF),
            jax.ShapeDtypeStruct((total, width), F32),
        ),
        in_specs=[pl.BlockSpec(memory_space=pl.ANY)] * 6,
        out_specs=(pl.BlockSpec(memory_space=pl.ANY),) * 4,
        scratch_shapes=[
            pltpu.VMEM((TICKS, 2, NY, NX, tokens, LANE), BF),
            pltpu.VMEM((TICKS, n_exp, 2, LANE, ff), BF),
            pltpu.VMEM((n_exp, slots, ff), BF),
            pltpu.VMEM((n_exp, slots, ff), F32),
            pltpu.VMEM((n_exp, slots, ff), BF),
            pltpu.VMEM((n_exp, slots, 2 * LANE), BF),
            pltpu.VMEM((NE // 2, n_exp * pair, 2 * LANE), BF),
            pltpu.VMEM((NE // 2, n_exp * pair, LANE), F32),
            pltpu.VMEM((NE, 16, LANE), F32),
            pltpu.VMEM((NE * n_exp, LANE), F32),
            pltpu.VMEM((NE * n_exp, LANE), F32),
            pltpu.VMEM((2, 2, n_exp, LANE, ff), BF),
            pltpu.VMEM((NE // 2, 8, 2 * LANE), F32),
            pltpu.VMEM((NE, 8, LANE), F32),
            pltpu.VMEM((NE, 8, LANE), F32),
            pltpu.VMEM((tokens, width), BF),
            pltpu.VMEM((total, width), BF),
            pltpu.VMEM((tokens, width), BF),
            pltpu.VMEM((total, width), F32),
            dma((TICKS, 2, 8)),
            dma((TICKS, 2, 8)),
            dma((TICKS, 2)),
            dma((TICKS, 2)),
            dma((4,)),
            dma((2, 2)),
            dma((n_exp,)),
            dma((2,)),
            dma((NE,)),
            dma((NE,)),
            dma((NE,)),
            dma((NE,)),
        ],
        compiler_params=pltpu.CompilerParams(
            collective_id=0, has_side_effects=True, vmem_limit_bytes=60 * 2**20
        ),
        name="moe_down_backward",
    )(meta, out_grad, hidden, down_weight, inputs, router_weight)
    down_grad = lax.psum_scatter(dw, "dp", scatter_dimension=1, tiled=True)
    router_grad = lax.psum(rp, ("dp", "expert"))
    return hg.reshape(saved_hidden.shape), down_grad, ig, router_grad


def solution(mesh):
    placed = (
        P(("dp", "expert"), None),
        P(("dp", "expert"), None),
        P(("dp", "expert"), None),
        P(("dp", "expert"), None),
        P("dp", "expert", None, None, None),
        P("expert", None, None),
        P(),
    )
    return jax.shard_map(
        local,
        mesh=mesh,
        in_specs=placed,
        out_specs=(
            P("dp", "expert", None, None, None),
            P("expert", "dp", None),
            P(("dp", "expert"), None),
            P(),
        ),
        check_vma=False,
    )
```

```python
import jax
import jax.numpy as jnp
from jax import lax
from jax.experimental import pallas as pl
from jax.experimental.pallas import tpu as pltpu
from jax.sharding import PartitionSpec as P

NX = 4
NY = 4
NZ = 4
NE = NX * NY
NDP = 2 * NZ
TICKS = 8
LANE = 128
BF = jnp.bfloat16
F32 = jnp.float32


def remote(src, dst, ssem, rsem, dev):
    return pltpu.make_async_remote_copy(
        src_ref=src, dst_ref=dst, send_sem=ssem, recv_sem=rsem,
        device_id=dev, device_id_type=pl.DeviceIdType.MESH,
    )


def fused(
    meta_hbm, og_hbm, hid_hbm, w_hbm, in_hbm, rw_hbm,
    hg_out, dw_out, ig_out, rp_out,
    G, W, H, HG, X, S, GAIN, META, CODES, GROW, RR, RSEND, RRECV,
    CS, CR, OWN, ZA, ZB, ZC, ZD, INP, RW, IG, RP, R1, R2, OUT,
    ag_s, ag_r, own_s, w_s, misc_s, hg_s, out_s, meta_s, meta_r, ret_s, ret_r,
    core_s, core_r, z_s, z_r, r1_s, r1_r, r2_s, r2_r, r3_s, r3_r,
):
    n_exp, slots, width_ff = hid_hbm.shape
    cap = slots // NE
    pair = 2 * cap
    me = lax.axis_index("expert")
    dp = lax.axis_index("dp")
    y, x = me // NX, lax.rem(me, NX)
    z, c = dp // 2, lax.rem(dp, 2)

    def expert_dev(index):
        return {"expert": index}

    def column(t, h):
        u = t // 2
        step = jnp.where(u == 0, 2, jnp.where(u == 1, 1, jnp.where(u == 2, 3, 0)))
        zz = lax.rem(z + step, NZ)
        core = 1 - c if h == 0 else c
        return pl.multiple_of((2 * zz + core) * 256 + lax.rem(t, 2) * LANE, LANE)

    def axes(h):
        return (x, y) if h == 0 else (y, x)

    def cell(t, h, a, b):
        return G.at[t, h, b, a] if h == 0 else G.at[t, h, a, b]

    def dev(h, a, b):
        return expert_dev(b * NX + a) if h == 0 else expert_dev(a * NX + b)

    def line(t, h, b, lo, n):
        return G.at[t, h, b, pl.ds(lo, n)] if h == 0 else G.at[t, h, pl.ds(lo, n), b]

    def up(i):
        return lax.rem(i + 1, 4)

    def down(i):
        return lax.rem(i + 3, 4)

    def far(i):
        return lax.rem(i + 2, 4)

    def hop(t, h, k):
        a, b = axes(h)
        if k == 0:
            return cell(t, h, a, b), cell(t, h, down(a), b), dev(h, up(a), b)
        if k == 1:
            return cell(t, h, a, b), cell(t, h, up(a), b), dev(h, down(a), b)
        if k == 2:
            lo = pl.ds(0, 64)
            return cell(t, h, down(a), b).at[lo], cell(t, h, far(a), b).at[lo], dev(h, up(a), b)
        if k == 3:
            hi = pl.ds(64, 64)
            return cell(t, h, up(a), b).at[hi], cell(t, h, far(a), b).at[hi], dev(h, down(a), b)
        if k == 4:
            return line(t, h, b, 0, 4), line(t, h, down(b), 0, 4), dev(h, a, up(b))
        if k == 5:
            return line(t, h, b, 0, 4), line(t, h, up(b), 0, 4), dev(h, a, down(b))
        if k == 6:
            return line(t, h, down(b), 0, 2), line(t, h, far(b), 0, 2), dev(h, a, up(b))
        return line(t, h, up(b), 2, 2), line(t, h, far(b), 2, 2), dev(h, a, down(b))

    def hop_start(t, h, k):
        sent, _, to = hop(t, h, k)
        remote(sent, sent, ag_s.at[t, h, k], ag_r.at[t, h, k], to).start()

    def hop_wait(t, h, k):
        _, got, to = hop(t, h, k)
        remote(got, got, ag_s.at[t, h, k], ag_r.at[t, h, k], to).wait_recv()

    def hop_drain(t, h, k):
        sent, _, to = hop(t, h, k)
        remote(sent, sent, ag_s.at[t, h, k], ag_r.at[t, h, k], to).wait_send()

    def own_copy(t, h):
        a, b = axes(h)
        return pltpu.make_async_copy(
            og_hbm.at[:, pl.ds(column(t, h), LANE)], cell(t, h, a, b), own_s.at[t, h]
        )

    def w_copy(t, h):
        return pltpu.make_async_copy(
            w_hbm.at[:, pl.ds(column(t, h), LANE), :], W.at[t, :, h], w_s.at[t, h]
        )

    def dp_dev(index):
        return {"dp": index}

    next_z = dp_dev(2 * lax.rem(z + 1, NZ) + c)
    prev_z = dp_dev(2 * lax.rem(z + 3, NZ) + c)

    def core_hop(t):
        return remote(
            CS.at[lax.rem(t, 2)], CR.at[t], core_s.at[t], core_r.at[t], dp_dev(2 * z + 1 - c)
        )

    def z_hop(v, k):
        t = v if k < 2 else (2 + v if k == 2 else 4 + v)
        if k == 0:
            sent, land = OWN.at[t, pl.ds(0, 2)], ZA.at[v]
        elif k == 1:
            sent, land = OWN.at[t, pl.ds(2, 2)], ZB.at[v]
        else:
            sent, land = OWN.at[t], (ZC.at[v] if k == 2 else ZD.at[v])
        return remote(sent, land, z_s.at[v, k], z_r.at[v, k], next_z if k in (0, 2) else prev_z)

    def add_blocks(t, lo, others):
        for e in range(lo, lo + 2):
            acc = OWN[t, e].astype(F32)
            for other in others(e):
                acc += other.astype(F32)
            OWN[t, e] = acc.astype(BF)

    def pair_up(t):
        core_hop(t).wait_recv()
        v, u = lax.rem(t, 2), t // 2

        @pl.when(u != 1)
        def _():
            add_blocks(t, 0, lambda e: [CR[t, e]])

        @pl.when(u == 1)
        def _():
            z_hop(v, 0).wait_recv()
            add_blocks(t, 0, lambda e: [CR[t, e], ZA[v, e]])

        @pl.when(u != 2)
        def _():
            add_blocks(t, 2, lambda e: [CR[t, e]])

        @pl.when(u == 2)
        def _():
            z_hop(v, 1).wait_recv()
            add_blocks(t, 2, lambda e: [CR[t, e], ZB[v, e - 2]])

        @pl.when(u == 0)
        def _():
            z_hop(v, 0).start()
            z_hop(v, 1).start()

        @pl.when(u == 1)
        def _():
            z_hop(v, 2).start()

        @pl.when(u == 2)
        def _():
            z_hop(v, 3).start()

    def dw_copy(v):
        return pltpu.make_async_copy(
            OWN.at[6 + v], dw_out.at[:, pl.ds(v * LANE, LANE), :], out_s.at[2 + v]
        )

    def finish_down(v):
        z_hop(v, 2).wait_recv()
        z_hop(v, 3).wait_recv()
        for lo in (0, 2):
            add_blocks(6 + v, lo, lambda e: [ZC[v, e], ZD[v, e]])
        dw_copy(v).start()

    meta_own = pltpu.make_async_copy(meta_hbm, META.at[me], misc_s.at[0])
    meta_own.start()
    for t in range(TICKS):
        for h in range(2):
            own_copy(t, h).start()
    hid_copy = pltpu.make_async_copy(hid_hbm, H, misc_s.at[1])
    in_copy = pltpu.make_async_copy(in_hbm, INP, misc_s.at[2])
    rw_copy = pltpu.make_async_copy(rw_hbm, RW, misc_s.at[3])

    barrier = pltpu.get_barrier_semaphore()
    for d in range(1, NE):
        pl.semaphore_signal(barrier, inc=1, device_id=expert_dev(lax.rem(me + d, NE)),
                            device_id_type=pl.DeviceIdType.MESH)
    for d in range(1, NDP):
        pl.semaphore_signal(barrier, inc=1, device_id=dp_dev(lax.rem(dp + d, NDP)),
                            device_id_type=pl.DeviceIdType.MESH)
    hid_copy.start()
    for t in range(TICKS):
        for h in range(2):
            w_copy(t, h).start()
    in_copy.start()
    rw_copy.start()
    pl.semaphore_wait(barrier, NE - 1 + NDP - 1)

    meta_own.wait()

    def plane_to(d):
        return expert_dev(lax.rem(me + d, NE))

    def plane_from(d):
        return lax.rem(me + NE - d, NE)

    def meta_send(d):
        return remote(META.at[me], META.at[me], meta_s.at[d], meta_r.at[d], plane_to(d))

    def meta_recv(d):
        got = META.at[plane_from(d)]
        return remote(got, got, meta_s.at[d], meta_r.at[d], plane_to(d))

    def build_dispatch():
        for d in range(1, NE):
            meta_recv(d).wait_recv()

        @pl.loop(0, NE // 2)
        def _(p):
            marks, gains = [], []
            for s2 in range(2):
                block = META[2 * p + s2]
                cb, rt = block[0:8], block[8:16]
                for e in range(n_exp):
                    hit = rt == (me * n_exp + e).astype(F32)
                    marks.append(jnp.sum(jnp.where(hit, 1.0, 0.0), axis=0, keepdims=True))
                    gains.append(jnp.sum(jnp.where(hit, cb, 0.0), axis=0, keepdims=True))
            at = pl.multiple_of(p * 8, 8)
            CODES[pl.ds(at, 8), :] = jnp.concatenate(marks, axis=0)
            GROW[pl.ds(at, 8), :] = jnp.concatenate(gains, axis=0)

        marks = CODES[...]
        r = lax.broadcasted_iota(jnp.int32, (LANE, LANE), 0)
        q = lax.broadcasted_iota(jnp.int32, (LANE, LANE), 1)
        earlier = jnp.where(r < q, 1.0, 0.0).astype(BF)
        before = jnp.dot(marks.astype(BF), earlier, preferred_element_type=F32)
        CODES[...] = jnp.where(marks > 0.5, before, -1000.0)

        @pl.loop(0, NE // 2)
        def _(p):
            at = pl.multiple_of(p * 8, 8)
            codes = CODES[pl.ds(at, 8), :]
            gains = GROW[pl.ds(at, 8), :]
            place = lax.broadcasted_iota(jnp.int32, (pair, LANE), 0).astype(F32)
            for e in range(n_exp):
                first = jnp.where(place == codes[e:e + 1], 1.0, 0.0)
                second = jnp.where(place - cap == codes[n_exp + e:n_exp + e + 1], 1.0, 0.0)
                S[p, e * pair:(e + 1) * pair, 0:LANE] = first.astype(BF)
                S[p, e * pair:(e + 1) * pair, LANE:2 * LANE] = second.astype(BF)
                gain = jnp.sum(
                    first * gains[e:e + 1] + second * gains[n_exp + e:n_exp + e + 1],
                    axis=1, keepdims=True,
                )
                GAIN[p, e * pair:(e + 1) * pair, :] = jnp.broadcast_to(gain, (pair, LANE))

    def compute(t):
        for h in range(2):
            w_copy(t, h).wait()
        for p in range(NE // 2):
            yy, xx = p // 2, 2 * (p % 2)
            g0 = G[t, 0, yy, xx:xx + 2].reshape(2 * LANE, LANE)
            g1 = G[t, 1, yy, xx:xx + 2].reshape(2 * LANE, LANE)
            rows = jnp.dot(S[p], jnp.concatenate([g0, g1], axis=1), preferred_element_type=F32)
            gain = GAIN[p]
            rows = (rows * jnp.concatenate([gain, gain], axis=1)).astype(BF)
            for e in range(n_exp):
                X[e, p * pair:(p + 1) * pair, :] = rows[e * pair:(e + 1) * pair]

        @pl.when(t >= 2)
        def _():
            core_hop(t - 2).wait_send()

        @pl.loop(0, n_exp)
        def _(e):
            xe = X[e]
            we = W[t, e].reshape(2 * LANE, width_ff)
            HG[e] += jnp.dot(xe, we, preferred_element_type=F32)
            grad = lax.dot_general(xe, H[e], (((0,), (0,)), ((), ())), preferred_element_type=F32)
            CS[lax.rem(t, 2), e] = grad[:LANE].astype(BF)
            OWN[t, e] = grad[LANE:].astype(BF)

        core_hop(t).start()

    @pl.loop(0, TICKS + 4)
    def _(i):
        @pl.when(i < TICKS)
        def _():
            for h in range(2):
                own_copy(i, h).wait()
                hop_start(i, h, 0)
                hop_start(i, h, 1)

        @pl.when(i == 0)
        def _():
            for d in range(1, NE):
                meta_send(d).start()
            hid_copy.wait()
            HG[...] = jnp.zeros_like(HG)

        for phase in range(3):
            @pl.when((i > phase) & (i <= TICKS + phase))
            def _(phase=phase):
                t = i - 1 - phase
                for h in range(2):
                    for k in (2 * phase, 2 * phase + 1):
                        hop_wait(t, h, k)
                        if phase != 1:
                            hop_start(t, h, k + 2)
                if phase == 1:
                    for h in range(2):
                        hop_start(t, h, 4)
                        hop_start(t, h, 5)

        @pl.when(i == 3)
        def _():
            build_dispatch()

        @pl.when(i >= 5)
        def _():
            pair_up(i - 5)

        @pl.when(i >= 4)
        def _():
            t = i - 4
            for h in range(2):
                hop_wait(t, h, 6)
                hop_wait(t, h, 7)
            compute(t)

    for e in range(n_exp):
        hg = HG[e]
        for q in range(3):
            W[e, q // 2, q % 2] = hg[q * LANE:(q + 1) * LANE].astype(BF)
        prod = jnp.sum(H[e].astype(F32) * hg, axis=1, keepdims=True)
        for p in range(NE // 2):
            row = jnp.sum(
                S[p, e * pair:(e + 1) * pair, :].astype(F32) * prod[p * pair:(p + 1) * pair],
                axis=0, keepdims=True,
            )
            RR[p, e:e + 1, :] = row
            RR[p, n_exp + e:n_exp + e + 1, :] = row
    half = lax.broadcasted_iota(jnp.int32, (8, LANE), 0) // n_exp
    mine = half == lax.rem(me, 2)
    for p in range(NE // 2):
        for s2 in range(2):
            RSEND[2 * p + s2] = jnp.where(mine, RR[p, :, s2 * LANE:(s2 + 1) * LANE], 0.0)

    def ret_send(d):
        out = RSEND.at[lax.rem(me + d, NE)]
        return remote(out, RRECV.at[me], ret_s.at[d], ret_r.at[d], plane_to(d))

    def ret_recv(d):
        got = RRECV.at[plane_from(d)]
        return remote(got, got, ret_s.at[d], ret_r.at[d], plane_to(d))

    for d in range(1, NE):
        ret_send(d).start()
    RRECV[me] = RSEND[me]

    def hg_copy(e, q):
        return pltpu.make_async_copy(
            W.at[e, q // 2, q % 2], hg_out.at[e, pl.ds(q * LANE, LANE)], hg_s.at[e, q]
        )

    for e in range(n_exp):
        for q in range(3):
            hg_copy(e, q).start()
    pair_up(TICKS - 1)

    own_meta = META[me]
    expert_id = lax.broadcasted_iota(jnp.int32, (NE * n_exp, LANE), 0).astype(F32)
    gate = jnp.zeros((NE * n_exp, LANE), F32)
    named = jnp.zeros((NE * n_exp, LANE), F32)
    for k in range(8):
        hit = expert_id == own_meta[8 + k:9 + k]
        gate += jnp.where(hit, own_meta[k:k + 1], 0.0)
        named += jnp.where(hit, 1.0, 0.0)

    in_copy.wait()
    rw_copy.wait()
    for d in range(1, NE):
        ret_recv(d).wait_recv()
    sums = jnp.concatenate([RRECV[2 * q] + RRECV[2 * q + 1] for q in range(NE // 2)], axis=0)
    total = jnp.sum(sums, axis=0, keepdims=True)
    dense = jnp.where(named > 0.5, sums - gate * total, 0.0).astype(BF)
    for q in range(4):
        cols = slice(q * 512, (q + 1) * 512)
        part = jnp.dot(dense, INP[:, cols], preferred_element_type=F32)
        for j in range(4):
            RP[4 * q + j] = part[:, j * LANE:(j + 1) * LANE]

    def r1_send(d):
        return remote(RP.at[lax.rem(me + d, NE)], R1.at[me], r1_s.at[d], r1_r.at[d], plane_to(d))

    def r1_recv(d):
        got = R1.at[plane_from(d)]
        return remote(got, got, r1_s.at[d], r1_r.at[d], plane_to(d))

    def r2_send(d):
        to = dp_dev(lax.rem(dp + d, NDP))
        return remote(R2.at[dp], R2.at[dp], r2_s.at[d], r2_r.at[d], to)

    def r2_recv(d):
        got = R2.at[lax.rem(dp + NDP - d, NDP)]
        return remote(got, got, r2_s.at[d], r2_r.at[d], dp_dev(lax.rem(dp + d, NDP)))

    def r3_send(d):
        return remote(OUT.at[me], OUT.at[me], r3_s.at[d], r3_r.at[d], plane_to(d))

    def r3_recv(d):
        got = OUT.at[plane_from(d)]
        return remote(got, got, r3_s.at[d], r3_r.at[d], plane_to(d))

    for d in range(1, NE):
        r1_send(d).start()
    R1[me] = RP[me]
    for q in range(4):
        cols = slice(q * 512, (q + 1) * 512)
        IG[:, cols] = lax.dot_general(
            dense, RW[:, cols], (((0,), (0,)), ((), ())), preferred_element_type=F32
        ).astype(BF)
    ig_copy = pltpu.make_async_copy(IG, ig_out, out_s.at[0])
    ig_copy.start()

    for d in range(1, NE):
        r1_recv(d).wait_recv()
    acc = R1[0]
    for j in range(1, NE):
        acc += R1[j]
    R2[dp] = acc
    for d in range(1, NDP):
        r2_send(d).start()
    finish_down(0)
    for d in range(1, NDP):
        r2_recv(d).wait_recv()
    acc = R2[0]
    for j in range(1, NDP):
        acc += R2[j]
    OUT[me] = acc
    for d in range(1, NE):
        r3_send(d).start()
    finish_down(1)
    for d in range(1, NE):
        r3_recv(d).wait_recv()

    def rp_copy(j):
        return pltpu.make_async_copy(
            OUT.at[j], rp_out.at[:, pl.ds(j * LANE, LANE)], misc_s.at[4 + j]
        )

    for j in range(NE):
        rp_copy(j).start()

    @pl.loop(0, TICKS)
    def _(t):
        for h in range(2):
            for k in range(8):
                hop_drain(t, h, k)

    for d in range(1, NE):
        meta_send(d).wait_send()
        ret_send(d).wait_send()
        r1_send(d).wait_send()
        r3_send(d).wait_send()
    for d in range(1, NDP):
        r2_send(d).wait_send()
    core_hop(TICKS - 2).wait_send()
    core_hop(TICKS - 1).wait_send()
    for v in range(2):
        for k in range(4):
            z_hop(v, k).wait_send()
        dw_copy(v).wait()
    for e in range(n_exp):
        for q in range(3):
            hg_copy(e, q).wait()
    ig_copy.wait()
    for j in range(NE):
        rp_copy(j).wait()


def local(inputs, out_grad, combine, routes, saved_hidden, down_weight, router_weight):
    tokens, width = out_grad.shape
    n_exp, _, ff = down_weight.shape
    total = router_weight.shape[0]
    slots = saved_hidden.shape[2] * saved_hidden.shape[3]
    pair = slots // (NE // 2)
    meta = jnp.concatenate([combine.T, routes.T.astype(F32)], axis=0)
    hidden = saved_hidden.reshape(n_exp, slots, ff)
    dma = pltpu.SemaphoreType.DMA
    hg, dw, ig, rp = pl.pallas_call(
        fused,
        out_shape=(
            jax.ShapeDtypeStruct((n_exp, slots, ff), BF),
            jax.ShapeDtypeStruct((n_exp, width // NDP, ff), BF),
            jax.ShapeDtypeStruct((tokens, width), BF),
            jax.ShapeDtypeStruct((total, width), F32),
        ),
        in_specs=[pl.BlockSpec(memory_space=pl.ANY)] * 6,
        out_specs=(pl.BlockSpec(memory_space=pl.ANY),) * 4,
        scratch_shapes=[
            pltpu.VMEM((TICKS, 2, NY, NX, tokens, LANE), BF),
            pltpu.VMEM((TICKS, n_exp, 2, LANE, ff), BF),
            pltpu.VMEM((n_exp, slots, ff), BF),
            pltpu.VMEM((n_exp, slots, ff), F32),
            pltpu.VMEM((n_exp, slots, 2 * LANE), BF),
            pltpu.VMEM((NE // 2, n_exp * pair, 2 * LANE), BF),
            pltpu.VMEM((NE // 2, n_exp * pair, LANE), F32),
            pltpu.VMEM((NE, 16, LANE), F32),
            pltpu.VMEM((NE * n_exp, LANE), F32),
            pltpu.VMEM((NE * n_exp, LANE), F32),
            pltpu.VMEM((NE // 2, 8, 2 * LANE), F32),
            pltpu.VMEM((NE, 8, LANE), F32),
            pltpu.VMEM((NE, 8, LANE), F32),
            pltpu.VMEM((2, n_exp, LANE, ff), BF),
            pltpu.VMEM((TICKS, n_exp, LANE, ff), BF),
            pltpu.VMEM((TICKS, n_exp, LANE, ff), BF),
            pltpu.VMEM((2, 2, LANE, ff), BF),
            pltpu.VMEM((2, 2, LANE, ff), BF),
            pltpu.VMEM((2, n_exp, LANE, ff), BF),
            pltpu.VMEM((2, n_exp, LANE, ff), BF),
            pltpu.VMEM((tokens, width), BF),
            pltpu.VMEM((total, width), BF),
            pltpu.VMEM((tokens, width), BF),
            pltpu.VMEM((NE, total, LANE), F32),
            pltpu.VMEM((NE, total, LANE), F32),
            pltpu.VMEM((NDP, total, LANE), F32),
            pltpu.VMEM((NE, total, LANE), F32),
            dma((TICKS, 2, 8)),
            dma((TICKS, 2, 8)),
            dma((TICKS, 2)),
            dma((TICKS, 2)),
            dma((4 + NE,)),
            dma((n_exp, 3)),
            dma((4,)),
            dma((NE,)),
            dma((NE,)),
            dma((NE,)),
            dma((NE,)),
            dma((TICKS,)),
            dma((TICKS,)),
            dma((2, 4)),
            dma((2, 4)),
            dma((NE,)),
            dma((NE,)),
            dma((NDP,)),
            dma((NDP,)),
            dma((NE,)),
            dma((NE,)),
        ],
        compiler_params=pltpu.CompilerParams(
            collective_id=0, has_side_effects=True, vmem_limit_bytes=60 * 2**20
        ),
        name="moe_down_backward",
    )(meta, out_grad, hidden, down_weight, inputs, router_weight)
    return hg.reshape(saved_hidden.shape), dw, ig, rp


def solution(mesh):
    placed = (
        P(("dp", "expert"), None),
        P(("dp", "expert"), None),
        P(("dp", "expert"), None),
        P(("dp", "expert"), None),
        P("dp", "expert", None, None, None),
        P("expert", None, None),
        P(),
    )
    return jax.shard_map(
        local,
        mesh=mesh,
        in_specs=placed,
        out_specs=(
            P("dp", "expert", None, None, None),
            P("expert", "dp", None),
            P(("dp", "expert"), None),
            P(),
        ),
        check_vma=False,
    )
```

```python
import jax
import jax.numpy as jnp
from jax import lax
from jax.experimental import pallas as pl
from jax.experimental.pallas import tpu as pltpu
from jax.sharding import PartitionSpec as P

NX = 4
NY = 4
NZ = 4
NE = NX * NY
NDP = 2 * NZ
TICKS = 8
LANE = 128
BF = jnp.bfloat16
F32 = jnp.float32


def remote(src, dst, ssem, rsem, dev):
    return pltpu.make_async_remote_copy(
        src_ref=src, dst_ref=dst, send_sem=ssem, recv_sem=rsem,
        device_id=dev, device_id_type=pl.DeviceIdType.MESH,
    )


def fused(
    comb_hbm, route_hbm, og_hbm, hid_hbm, w_hbm, in_hbm, rw_hbm,
    hg_out, dw_out, ig_out, rp_out,
    G, W, H, HG, X, S, GAIN, META, ROUTE, CODES, GROW, RR, RSEND, RRECV,
    CS, CR, OWN, ZA, ZB, ZC, ZD, INP, RW, IG, RP, RC, R1, R2, OUT,
    ag_s, ag_r, own_s, w_s, misc_s, hg_s, out_s, meta_s, meta_r, ret_s, ret_r,
    core_s, core_r, z_s, z_r, r1_s, r1_r, r2_s, r2_r, r3_s, r3_r, rc_s, rc_r, rp_s,
):
    n_exp, slots, width_ff = hid_hbm.shape
    cap = slots // NE
    pair = 2 * cap
    me = lax.axis_index("expert")
    dp = lax.axis_index("dp")
    y, x = me // NX, lax.rem(me, NX)
    z, c = dp // 2, lax.rem(dp, 2)

    def expert_dev(index):
        return {"expert": index}

    def column(t, h):
        step = jnp.where(t < 2, 2, jnp.where(t >= 6, 0, 1 + 2 * lax.rem(t, 2)))
        v = jnp.where(t < 2, t, jnp.where(t >= 6, t - 6, (t - 2) // 2))
        zz = lax.rem(z + step, NZ)
        core = 1 - c if h == 0 else c
        return pl.multiple_of((2 * zz + core) * 256 + v * LANE, LANE)

    def axes(h):
        return (x, y) if h == 0 else (y, x)

    def cell(t, h, a, b):
        return G.at[t, h, b, a] if h == 0 else G.at[t, h, a, b]

    def dev(h, a, b):
        return expert_dev(b * NX + a) if h == 0 else expert_dev(a * NX + b)

    def line(t, h, b, lo, n):
        return G.at[t, h, b, pl.ds(lo, n)] if h == 0 else G.at[t, h, pl.ds(lo, n), b]

    def up(i):
        return lax.rem(i + 1, 4)

    def down(i):
        return lax.rem(i + 3, 4)

    def far(i):
        return lax.rem(i + 2, 4)

    def hop(t, h, k):
        a, b = axes(h)
        if k == 0:
            return cell(t, h, a, b), cell(t, h, down(a), b), dev(h, up(a), b)
        if k == 1:
            return cell(t, h, a, b), cell(t, h, up(a), b), dev(h, down(a), b)
        if k == 2:
            lo = pl.ds(0, 64)
            return cell(t, h, down(a), b).at[lo], cell(t, h, far(a), b).at[lo], dev(h, up(a), b)
        if k == 3:
            hi = pl.ds(64, 64)
            return cell(t, h, up(a), b).at[hi], cell(t, h, far(a), b).at[hi], dev(h, down(a), b)
        if k == 4:
            return line(t, h, b, 0, 4), line(t, h, down(b), 0, 4), dev(h, a, up(b))
        if k == 5:
            return line(t, h, b, 0, 4), line(t, h, up(b), 0, 4), dev(h, a, down(b))
        if k == 6:
            return line(t, h, down(b), 0, 2), line(t, h, far(b), 0, 2), dev(h, a, up(b))
        return line(t, h, up(b), 2, 2), line(t, h, far(b), 2, 2), dev(h, a, down(b))

    def hop_start(t, h, k):
        sent, _, to = hop(t, h, k)
        remote(sent, sent, ag_s.at[t, h, k], ag_r.at[t, h, k], to).start()

    def hop_wait(t, h, k):
        _, got, to = hop(t, h, k)
        remote(got, got, ag_s.at[t, h, k], ag_r.at[t, h, k], to).wait_recv()

    def hop_drain(t, h, k):
        sent, _, to = hop(t, h, k)
        remote(sent, sent, ag_s.at[t, h, k], ag_r.at[t, h, k], to).wait_send()

    def own_copy(t, h):
        a, b = axes(h)
        return pltpu.make_async_copy(
            og_hbm.at[:, pl.ds(column(t, h), LANE)], cell(t, h, a, b), own_s.at[t, h]
        )

    def w_copy(t, h):
        return pltpu.make_async_copy(
            w_hbm.at[:, pl.ds(column(t, h), LANE), :], W.at[t, :, h], w_s.at[t, h]
        )

    def dp_dev(index):
        return {"dp": index}

    next_z = dp_dev(2 * lax.rem(z + 1, NZ) + c)
    prev_z = dp_dev(2 * lax.rem(z + 3, NZ) + c)

    def core_hop(t, e):
        return remote(
            CS.at[lax.rem(t, 2), e], CR.at[t, e], core_s.at[t, e], core_r.at[t, e],
            dp_dev(2 * z + 1 - c),
        )

    def z_hop(v, k):
        t = v if k < 2 else k + 2 * v
        if k == 0:
            sent, land = OWN.at[t, pl.ds(0, 2)], ZA.at[v]
        elif k == 1:
            sent, land = OWN.at[t, pl.ds(2, 2)], ZB.at[v]
        else:
            sent, land = OWN.at[t], (ZC.at[v] if k == 2 else ZD.at[v])
        return remote(sent, land, z_s.at[v, k], z_r.at[v, k], next_z if k in (0, 2) else prev_z)

    def add_blocks(t, lo, others):
        for e in range(lo, lo + 2):
            acc = OWN[t, e].astype(F32)
            for other in others(e):
                acc += other.astype(F32)
            OWN[t, e] = acc.astype(BF)

    def core_wait(t, lo):
        for e in (lo, lo + 1):
            core_hop(t, e).wait_recv()

    def pair_up(t):
        @pl.when(t < 2)
        def _():
            for k in range(2):
                core_wait(t, 2 * k)
                add_blocks(t, 2 * k, lambda e: [CR[t, e]])
                z_hop(t, k).start()

        @pl.when((t == 2) | (t == 4))
        def _():
            v = (t - 2) // 2
            z_hop(v, 0).wait_recv()
            core_wait(t, 0)
            add_blocks(t, 0, lambda e: [CR[t, e], ZA[v, e]])
            core_wait(t, 2)
            add_blocks(t, 2, lambda e: [CR[t, e]])
            z_hop(v, 2).start()

        @pl.when((t == 3) | (t == 5))
        def _():
            v = (t - 2) // 2
            core_wait(t, 0)
            add_blocks(t, 0, lambda e: [CR[t, e]])
            z_hop(v, 1).wait_recv()
            core_wait(t, 2)
            add_blocks(t, 2, lambda e: [CR[t, e], ZB[v, e - 2]])
            z_hop(v, 3).start()

    def dw_copy(v):
        return pltpu.make_async_copy(
            OWN.at[6 + v], dw_out.at[:, pl.ds(v * LANE, LANE), :], out_s.at[2 + v]
        )

    def finish_down(v):
        z_hop(v, 2).wait_recv()
        z_hop(v, 3).wait_recv()
        for lo in (0, 2):
            core_wait(6 + v, lo)
            add_blocks(6 + v, lo, lambda e: [CR[6 + v, e], ZC[v, e], ZD[v, e]])
        dw_copy(v).start()

    comb_own = pltpu.make_async_copy(comb_hbm, META.at[me, pl.ds(0, 8)], misc_s.at[0])
    route_own = pltpu.make_async_copy(route_hbm, ROUTE, misc_s.at[4])
    comb_own.start()
    route_own.start()
    for t in range(TICKS):
        for h in range(2):
            own_copy(t, h).start()
    hid_copy = pltpu.make_async_copy(hid_hbm, H, misc_s.at[1])
    in_copy = pltpu.make_async_copy(in_hbm, INP, misc_s.at[2])
    rw_copy = pltpu.make_async_copy(rw_hbm, RW, misc_s.at[3])

    barrier = pltpu.get_barrier_semaphore()
    for d in range(1, NE):
        pl.semaphore_signal(barrier, inc=1, device_id=expert_dev(lax.rem(me + d, NE)),
                            device_id_type=pl.DeviceIdType.MESH)
    for d in range(1, NDP):
        pl.semaphore_signal(barrier, inc=1, device_id=dp_dev(lax.rem(dp + d, NDP)),
                            device_id_type=pl.DeviceIdType.MESH)
    hid_copy.start()
    for t in range(TICKS):
        for h in range(2):
            w_copy(t, h).start()
    in_copy.start()
    rw_copy.start()
    comb_own.wait()
    route_own.wait()
    META[me, 8:16, :] = ROUTE[...].astype(F32)
    pl.semaphore_wait(barrier, NE - 1 + NDP - 1)

    def plane_to(d):
        return expert_dev(lax.rem(me + d, NE))

    def plane_from(d):
        return lax.rem(me + NE - d, NE)

    def meta_send(d):
        return remote(META.at[me], META.at[me], meta_s.at[d], meta_r.at[d], plane_to(d))

    def meta_recv(d):
        got = META.at[plane_from(d)]
        return remote(got, got, meta_s.at[d], meta_r.at[d], plane_to(d))

    def build_codes():
        for d in range(1, NE):
            meta_recv(d).wait_recv()

        for p in range(NE // 2):
            marks, gains = [], []
            for s2 in range(2):
                block = META[2 * p + s2]
                cb, rt = block[0:8], block[8:16]
                for e in range(n_exp):
                    hit = rt == (me * n_exp + e).astype(F32)
                    marks.append(jnp.sum(jnp.where(hit, 1.0, 0.0), axis=0, keepdims=True))
                    gains.append(jnp.sum(jnp.where(hit, cb, 0.0), axis=0, keepdims=True))
            CODES[8 * p:8 * p + 8, :] = jnp.concatenate(marks, axis=0)
            GROW[8 * p:8 * p + 8, :] = jnp.concatenate(gains, axis=0)

        marks = CODES[...]
        r = lax.broadcasted_iota(jnp.int32, (LANE, LANE), 0)
        q = lax.broadcasted_iota(jnp.int32, (LANE, LANE), 1)
        earlier = jnp.where(r < q, 1.0, 0.0).astype(BF)
        before = jnp.dot(marks.astype(BF), earlier, preferred_element_type=F32)
        CODES[...] = jnp.where(marks > 0.5, before, -1000.0)

    def build_dispatch():
        place = lax.broadcasted_iota(jnp.int32, (pair, LANE), 0).astype(F32)
        for p in range(NE // 2):
            codes = CODES[8 * p:8 * p + 8, :]
            gains = GROW[8 * p:8 * p + 8, :]
            for e in range(n_exp):
                first = jnp.where(place == codes[e:e + 1], 1.0, 0.0)
                second = jnp.where(place - cap == codes[n_exp + e:n_exp + e + 1], 1.0, 0.0)
                S[p, e * pair:(e + 1) * pair, 0:LANE] = first.astype(BF)
                S[p, e * pair:(e + 1) * pair, LANE:2 * LANE] = second.astype(BF)
                gain = jnp.sum(
                    first * gains[e:e + 1] + second * gains[n_exp + e:n_exp + e + 1],
                    axis=1, keepdims=True,
                )
                GAIN[p, e * pair:(e + 1) * pair, :] = jnp.broadcast_to(gain, (pair, LANE))

    def compute(t):
        for h in range(2):
            w_copy(t, h).wait()
        for p in range(NE // 2):
            yy, xx = p // 2, 2 * (p % 2)
            g0 = G[t, 0, yy, xx:xx + 2].reshape(2 * LANE, LANE)
            g1 = G[t, 1, yy, xx:xx + 2].reshape(2 * LANE, LANE)
            rows = jnp.dot(S[p], jnp.concatenate([g0, g1], axis=1), preferred_element_type=F32)
            gain = GAIN[p]
            rows = (rows * jnp.concatenate([gain, gain], axis=1)).astype(BF)
            for e in range(n_exp):
                X[e, p * pair:(p + 1) * pair, :] = rows[e * pair:(e + 1) * pair]

        @pl.loop(0, n_exp)
        def _(e):
            xe = X[e]
            we = W[t, e].reshape(2 * LANE, width_ff)
            HG[e] += jnp.dot(xe, we, preferred_element_type=F32)
            grad = lax.dot_general(xe, H[e], (((0,), (0,)), ((), ())), preferred_element_type=F32)

            @pl.when(t >= 2)
            def _():
                core_hop(t - 2, e).wait_send()

            CS[lax.rem(t, 2), e] = grad[:LANE].astype(BF)
            core_hop(t, e).start()
            OWN[t, e] = grad[LANE:].astype(BF)

            @pl.when(e == 0)
            def _():
                gather_ahead(t)

    def phase_start(t, phase):
        for h in range(2):
            if phase == 0:
                own_copy(t, h).wait()
            hop_start(t, h, 2 * phase)
            hop_start(t, h, 2 * phase + 1)

    def phase_wait(t, phase):
        for h in range(2):
            hop_wait(t, h, 2 * phase)
            hop_wait(t, h, 2 * phase + 1)

    def gather_ahead(t):
        @pl.when(t + 1 < TICKS)
        def _():
            phase_wait(t + 1, 2)
            phase_start(t + 1, 3)

        @pl.when(t + 3 < TICKS)
        def _():
            phase_wait(t + 3, 1)
            phase_start(t + 3, 2)

        @pl.when(t + 5 < TICKS)
        def _():
            phase_wait(t + 5, 0)
            phase_start(t + 5, 1)

        @pl.when(t + 7 < TICKS)
        def _():
            phase_start(t + 7, 0)

    phase_start(0, 0)
    phase_start(1, 0)
    for d in range(1, NE):
        meta_send(d).start()
    phase_wait(0, 0)
    phase_start(0, 1)
    phase_start(2, 0)
    phase_wait(0, 1)
    phase_start(0, 2)
    phase_wait(1, 0)
    phase_start(1, 1)
    phase_start(3, 0)
    HG[...] = jnp.zeros_like(HG)
    build_codes()
    phase_wait(2, 0)
    phase_start(2, 1)
    phase_start(4, 0)
    phase_wait(0, 2)
    phase_start(0, 3)
    phase_wait(1, 1)
    phase_start(1, 2)
    phase_start(5, 0)
    phase_wait(3, 0)
    phase_start(3, 1)
    build_dispatch()
    phase_wait(2, 1)
    phase_start(2, 2)
    phase_wait(4, 0)
    phase_start(4, 1)
    phase_start(6, 0)
    hid_copy.wait()

    @pl.loop(0, TICKS)
    def _(t):
        phase_wait(t, 3)
        compute(t)

        @pl.when(t < 6)
        def _():
            pair_up(t)

    for e in range(n_exp):
        hg = HG[e]
        for q in range(3):
            W[e, q // 2, q % 2] = hg[q * LANE:(q + 1) * LANE].astype(BF)
        prod = jnp.sum(H[e].astype(F32) * hg, axis=1, keepdims=True)
        for p in range(NE // 2):
            row = jnp.sum(
                S[p, e * pair:(e + 1) * pair, :].astype(F32) * prod[p * pair:(p + 1) * pair],
                axis=0, keepdims=True,
            )
            RR[p, e:e + 1, :] = row
            RR[p, n_exp + e:n_exp + e + 1, :] = row
    half = lax.broadcasted_iota(jnp.int32, (8, LANE), 0) // n_exp
    mine = half == lax.rem(me, 2)
    for p in range(NE // 2):
        for s2 in range(2):
            RSEND[2 * p + s2] = jnp.where(mine, RR[p, :, s2 * LANE:(s2 + 1) * LANE], 0.0)

    def ret_send(d):
        out = RSEND.at[lax.rem(me + d, NE)]
        return remote(out, RRECV.at[me], ret_s.at[d], ret_r.at[d], plane_to(d))

    def ret_recv(d):
        got = RRECV.at[plane_from(d)]
        return remote(got, got, ret_s.at[d], ret_r.at[d], plane_to(d))

    for d in range(1, NE):
        ret_send(d).start()
    RRECV[me] = RSEND[me]

    def hg_copy(e, q):
        return pltpu.make_async_copy(
            W.at[e, q // 2, q % 2], hg_out.at[e, pl.ds(q * LANE, LANE)], hg_s.at[e, q]
        )

    for e in range(n_exp):
        for q in range(3):
            hg_copy(e, q).start()

    own_meta = META[me]
    expert_id = lax.broadcasted_iota(jnp.int32, (NE * n_exp, LANE), 0).astype(F32)
    gate = jnp.zeros((NE * n_exp, LANE), F32)
    named = jnp.zeros((NE * n_exp, LANE), F32)
    for k in range(8):
        hit = expert_id == own_meta[8 + k:9 + k]
        gate += jnp.where(hit, own_meta[k:k + 1], 0.0)
        named += jnp.where(hit, 1.0, 0.0)

    in_copy.wait()
    rw_copy.wait()
    for d in range(1, NE):
        ret_recv(d).wait_recv()
    sums = jnp.concatenate([RRECV[2 * q] + RRECV[2 * q + 1] for q in range(NE // 2)], axis=0)
    total = jnp.sum(sums, axis=0, keepdims=True)
    dense = jnp.where(named > 0.5, sums - gate * total, 0.0).astype(BF)
    rows_half = NE * n_exp // 2
    for q in range(4):
        cols = slice(q * 512, (q + 1) * 512)
        part = jnp.dot(dense, INP[:, cols], preferred_element_type=F32)
        for j in range(4):
            block = part[:, j * LANE:(j + 1) * LANE]
            RP[4 * q + j, 0] = block[:rows_half]
            RP[4 * q + j, 1] = block[rows_half:]

    other = dp_dev(2 * z + 1 - c)

    def rc_send():
        return remote(RP.at[:, 1 - c], RC, rc_s.at[0], rc_r.at[0], other)

    def r1_send(d):
        out = RP.at[lax.rem(me + d, NE), c]
        return remote(out, R1.at[me], r1_s.at[d], r1_r.at[d], plane_to(d))

    def r1_recv(d):
        got = R1.at[plane_from(d)]
        return remote(got, got, r1_s.at[d], r1_r.at[d], plane_to(d))

    def r2_send(d):
        to = dp_dev(2 * lax.rem(z + d, NZ) + c)
        return remote(R2.at[z], R2.at[z], r2_s.at[d], r2_r.at[d], to)

    def r2_recv(d):
        got = R2.at[lax.rem(z + NZ - d, NZ)]
        return remote(got, got, r2_s.at[d], r2_r.at[d], dp_dev(2 * lax.rem(z + d, NZ) + c))

    def r3_send(d):
        return remote(OUT.at[me, c], OUT.at[me, c], r3_s.at[d], r3_r.at[d], plane_to(d))

    def r3_recv(d):
        got = OUT.at[plane_from(d), c]
        return remote(got, got, r3_s.at[d], r3_r.at[d], plane_to(d))

    def r4_send():
        return remote(OUT.at[:, c], OUT.at[:, c], rc_s.at[1], rc_r.at[1], other)

    def r4_recv():
        return remote(OUT.at[:, 1 - c], OUT.at[:, 1 - c], rc_s.at[1], rc_r.at[1], other)

    rc_send().start()
    rc_send().wait_recv()
    for j in range(NE):
        RP[j, c] += RC[j]
    for d in range(1, NE):
        r1_send(d).start()
    R1[me] = RP[me, c]
    for q in range(4):
        cols = slice(q * 512, (q + 1) * 512)
        IG[:, cols] = lax.dot_general(
            dense, RW[:, cols], (((0,), (0,)), ((), ())), preferred_element_type=F32
        ).astype(BF)
    ig_copy = pltpu.make_async_copy(IG, ig_out, out_s.at[0])
    ig_copy.start()

    for d in range(1, NE):
        r1_recv(d).wait_recv()
    acc = R1[0]
    for j in range(1, NE):
        acc += R1[j]
    R2[z] = acc
    for d in range(1, NZ):
        r2_send(d).start()
    finish_down(0)
    for d in range(1, NZ):
        r2_recv(d).wait_recv()
    acc = R2[0]
    for j in range(1, NZ):
        acc += R2[j]
    OUT[me, c] = acc
    for d in range(1, NE):
        r3_send(d).start()
    finish_down(1)
    for d in range(1, NE):
        r3_recv(d).wait_recv()
    r4_send().start()
    r4_recv().wait_recv()

    def rp_copy(j, half):
        return pltpu.make_async_copy(
            OUT.at[j, half],
            rp_out.at[pl.ds(half * rows_half, rows_half), pl.ds(j * LANE, LANE)],
            rp_s.at[j, half],
        )

    for j in range(NE):
        rp_copy(j, 0).start()
        rp_copy(j, 1).start()

    @pl.loop(0, TICKS)
    def _(t):
        for h in range(2):
            for k in range(8):
                hop_drain(t, h, k)

    for d in range(1, NE):
        meta_send(d).wait_send()
        ret_send(d).wait_send()
        r1_send(d).wait_send()
        r3_send(d).wait_send()
    for d in range(1, NZ):
        r2_send(d).wait_send()
    rc_send().wait_send()
    r4_send().wait_send()
    for e in range(n_exp):
        core_hop(TICKS - 2, e).wait_send()
        core_hop(TICKS - 1, e).wait_send()
    for v in range(2):
        for k in range(4):
            z_hop(v, k).wait_send()
        dw_copy(v).wait()
    for e in range(n_exp):
        for q in range(3):
            hg_copy(e, q).wait()
    ig_copy.wait()
    for j in range(NE):
        rp_copy(j, 0).wait()
        rp_copy(j, 1).wait()


def local(inputs, out_grad, combine, routes, saved_hidden, down_weight, router_weight):
    tokens, width = out_grad.shape
    n_exp, _, ff = down_weight.shape
    total = router_weight.shape[0]
    slots = saved_hidden.shape[2] * saved_hidden.shape[3]
    pair = slots // (NE // 2)
    hidden = saved_hidden.reshape(n_exp, slots, ff)
    dma = pltpu.SemaphoreType.DMA
    hg, dw, ig, rp = pl.pallas_call(
        fused,
        out_shape=(
            pltpu.VMEM((n_exp, slots, ff), BF),
            pltpu.VMEM((n_exp, width // NDP, ff), BF),
            pltpu.VMEM((tokens, width), BF),
            pltpu.VMEM((total, width), F32),
        ),
        in_specs=[pl.BlockSpec(memory_space=pl.ANY)] * 7,
        out_specs=(pl.BlockSpec(memory_space=pltpu.VMEM),) * 4,
        scratch_shapes=[
            pltpu.VMEM((TICKS, 2, NY, NX, tokens, LANE), BF),
            pltpu.VMEM((TICKS, n_exp, 2, LANE, ff), BF),
            pltpu.VMEM((n_exp, slots, ff), BF),
            pltpu.VMEM((n_exp, slots, ff), F32),
            pltpu.VMEM((n_exp, slots, 2 * LANE), BF),
            pltpu.VMEM((NE // 2, n_exp * pair, 2 * LANE), BF),
            pltpu.VMEM((NE // 2, n_exp * pair, LANE), F32),
            pltpu.VMEM((NE, 16, LANE), F32),
            pltpu.VMEM((8, LANE), jnp.int32),
            pltpu.VMEM((NE * n_exp, LANE), F32),
            pltpu.VMEM((NE * n_exp, LANE), F32),
            pltpu.VMEM((NE // 2, 8, 2 * LANE), F32),
            pltpu.VMEM((NE, 8, LANE), F32),
            pltpu.VMEM((NE, 8, LANE), F32),
            pltpu.VMEM((2, n_exp, LANE, ff), BF),
            pltpu.VMEM((TICKS, n_exp, LANE, ff), BF),
            pltpu.VMEM((TICKS, n_exp, LANE, ff), BF),
            pltpu.VMEM((2, 2, LANE, ff), BF),
            pltpu.VMEM((2, 2, LANE, ff), BF),
            pltpu.VMEM((2, n_exp, LANE, ff), BF),
            pltpu.VMEM((2, n_exp, LANE, ff), BF),
            pltpu.VMEM((tokens, width), BF),
            pltpu.VMEM((total, width), BF),
            pltpu.VMEM((tokens, width), BF),
            pltpu.VMEM((NE, 2, total // 2, LANE), F32),
            pltpu.VMEM((NE, total // 2, LANE), F32),
            pltpu.VMEM((NE, total // 2, LANE), F32),
            pltpu.VMEM((NZ, total // 2, LANE), F32),
            pltpu.VMEM((NE, 2, total // 2, LANE), F32),
            dma((TICKS, 2, 8)),
            dma((TICKS, 2, 8)),
            dma((TICKS, 2)),
            dma((TICKS, 2)),
            dma((5,)),
            dma((n_exp, 3)),
            dma((4,)),
            dma((NE,)),
            dma((NE,)),
            dma((NE,)),
            dma((NE,)),
            dma((TICKS, n_exp)),
            dma((TICKS, n_exp)),
            dma((2, 4)),
            dma((2, 4)),
            dma((NE,)),
            dma((NE,)),
            dma((NZ,)),
            dma((NZ,)),
            dma((NE,)),
            dma((NE,)),
            dma((2,)),
            dma((2,)),
            dma((NE, 2)),
        ],
        compiler_params=pltpu.CompilerParams(
            collective_id=0, has_side_effects=True, vmem_limit_bytes=58 * 2**20
        ),
        name="moe_down_backward",
    )(combine.T, routes.T, out_grad, hidden, down_weight, inputs, router_weight)
    return hg.reshape(saved_hidden.shape), dw, ig, rp


def solution(mesh):
    placed = (
        P(("dp", "expert"), None),
        P(("dp", "expert"), None),
        P(("dp", "expert"), None),
        P(("dp", "expert"), None),
        P("dp", "expert", None, None, None),
        P("expert", None, None),
        P(),
    )
    return jax.shard_map(
        local,
        mesh=mesh,
        in_specs=placed,
        out_specs=(
            P("dp", "expert", None, None, None),
            P("expert", "dp", None),
            P(("dp", "expert"), None),
            P(),
        ),
        check_vma=False,
    )
```

```python
import jax
import jax.numpy as jnp
from jax import lax
from jax.experimental import pallas as pl
from jax.experimental.pallas import tpu as pltpu
from jax.sharding import PartitionSpec as P

NX = 4
NY = 4
NZ = 4
NE = NX * NY
NDP = 2 * NZ
TICKS = 8
LANE = 128
BF = jnp.bfloat16
F32 = jnp.float32


def remote(src, dst, ssem, rsem, dev):
    return pltpu.make_async_remote_copy(
        src_ref=src, dst_ref=dst, send_sem=ssem, recv_sem=rsem,
        device_id=dev, device_id_type=pl.DeviceIdType.MESH,
    )


def fused(
    comb_hbm, route_hbm, og_hbm, hid_hbm, w_hbm, in_hbm, rw_hbm,
    hg_out, dw_out, ig_out, rp_out,
    G, W, H, HG, X, S, GAIN, META, ROUTE, CODES, GROW, CS, CR, OWN, ZA, ZB, ZC, ZD,
    INP, INC, RW, GATE, PROD, PSB, SUMS, DENSE, PF, R2, OUT,
    ag_s, ag_r, own_s, w_s, misc_s, meta_s, meta_r, core_s, core_r, z_s, z_r,
    inc_s, inc_r, ps_s, ps_r, r2_s, r2_r, r3_s, r3_r, r4_s, r4_r,
):
    n_exp, slots, width_ff = hid_hbm.shape
    cap = slots // NE
    pair = 2 * cap
    me = lax.axis_index("expert")
    dp = lax.axis_index("dp")
    y, x = me // NX, lax.rem(me, NX)
    z, c = dp // 2, lax.rem(dp, 2)

    def expert_dev(index):
        return {"expert": index}

    def column(t, h):
        step = jnp.where(t < 2, 2, jnp.where(t >= 6, 0, 1 + 2 * lax.rem(t, 2)))
        v = jnp.where(t < 2, t, jnp.where(t >= 6, t - 6, (t - 2) // 2))
        zz = lax.rem(z + step, NZ)
        core = 1 - c if h == 0 else c
        return pl.multiple_of((2 * zz + core) * 256 + v * LANE, LANE)

    def axes(h):
        return (x, y) if h == 0 else (y, x)

    def cell(t, h, a, b):
        return G.at[t, h, b, a] if h == 0 else G.at[t, h, a, b]

    def dev(h, a, b):
        return expert_dev(b * NX + a) if h == 0 else expert_dev(a * NX + b)

    def line(t, h, b, lo, n):
        return G.at[t, h, b, pl.ds(lo, n)] if h == 0 else G.at[t, h, pl.ds(lo, n), b]

    def up(i):
        return lax.rem(i + 1, 4)

    def down(i):
        return lax.rem(i + 3, 4)

    def far(i):
        return lax.rem(i + 2, 4)

    def hop(t, h, k):
        a, b = axes(h)
        if k == 0:
            return cell(t, h, a, b), cell(t, h, down(a), b), dev(h, up(a), b)
        if k == 1:
            return cell(t, h, a, b), cell(t, h, up(a), b), dev(h, down(a), b)
        if k == 2:
            lo = pl.ds(0, 64)
            return cell(t, h, down(a), b).at[lo], cell(t, h, far(a), b).at[lo], dev(h, up(a), b)
        if k == 3:
            hi = pl.ds(64, 64)
            return cell(t, h, up(a), b).at[hi], cell(t, h, far(a), b).at[hi], dev(h, down(a), b)
        if k == 4:
            return line(t, h, b, 0, 4), line(t, h, down(b), 0, 4), dev(h, a, up(b))
        if k == 5:
            return line(t, h, b, 0, 4), line(t, h, up(b), 0, 4), dev(h, a, down(b))
        if k == 6:
            return line(t, h, down(b), 0, 2), line(t, h, far(b), 0, 2), dev(h, a, up(b))
        return line(t, h, up(b), 2, 2), line(t, h, far(b), 2, 2), dev(h, a, down(b))

    def hop_start(t, h, k):
        sent, _, to = hop(t, h, k)
        remote(sent, sent, ag_s.at[t, h, k], ag_r.at[t, h, k], to).start()

    def hop_wait(t, h, k):
        _, got, to = hop(t, h, k)
        remote(got, got, ag_s.at[t, h, k], ag_r.at[t, h, k], to).wait_recv()

    def hop_drain(t, h, k):
        sent, _, to = hop(t, h, k)
        remote(sent, sent, ag_s.at[t, h, k], ag_r.at[t, h, k], to).wait_send()

    def own_copy(t, h):
        a, b = axes(h)
        return pltpu.make_async_copy(
            og_hbm.at[:, pl.ds(column(t, h), LANE)], cell(t, h, a, b), own_s.at[t, h]
        )

    def w_copy(t, h):
        return pltpu.make_async_copy(
            w_hbm.at[:, pl.ds(column(t, h), LANE), :], W.at[t, :, h], w_s.at[t, h]
        )

    def dp_dev(index):
        return {"dp": index}

    next_z = dp_dev(2 * lax.rem(z + 1, NZ) + c)
    prev_z = dp_dev(2 * lax.rem(z + 3, NZ) + c)

    def core_hop(t, e):
        return remote(
            CS.at[lax.rem(t, 2), e], CR.at[t, e], core_s.at[t, e], core_r.at[t, e],
            dp_dev(2 * z + 1 - c),
        )

    def z_hop(v, k):
        t = v if k < 2 else k + 2 * v
        if k == 0:
            sent, land = OWN.at[t, pl.ds(0, 2)], ZA.at[v]
        elif k == 1:
            sent, land = OWN.at[t, pl.ds(2, 2)], ZB.at[v]
        else:
            sent, land = OWN.at[t], (ZC.at[v] if k == 2 else ZD.at[v])
        return remote(sent, land, z_s.at[v, k], z_r.at[v, k], next_z if k in (0, 2) else prev_z)

    def add_blocks(t, lo, others, into=None):
        for e in range(lo, lo + 2):
            acc = OWN[t, e].astype(F32)
            for other in others(e):
                acc += other.astype(F32)
            if into is None:
                OWN[t, e] = acc.astype(BF)
            else:
                dw_out[e, into * LANE:(into + 1) * LANE, :] = acc.astype(BF)

    def core_wait(t, lo):
        for e in (lo, lo + 1):
            core_hop(t, e).wait_recv()

    def pair_up(t):
        @pl.when(t < 2)
        def _():
            for k in range(2):
                core_wait(t, 2 * k)
                add_blocks(t, 2 * k, lambda e: [CR[t, e]])
                z_hop(t, k).start()

        @pl.when((t == 2) | (t == 4))
        def _():
            v = (t - 2) // 2
            z_hop(v, 0).wait_recv()
            core_wait(t, 0)
            add_blocks(t, 0, lambda e: [CR[t, e], ZA[v, e]])
            core_wait(t, 2)
            add_blocks(t, 2, lambda e: [CR[t, e]])
            z_hop(v, 2).start()

        @pl.when((t == 3) | (t == 5))
        def _():
            v = (t - 2) // 2
            core_wait(t, 0)
            add_blocks(t, 0, lambda e: [CR[t, e]])
            z_hop(v, 1).wait_recv()
            core_wait(t, 2)
            add_blocks(t, 2, lambda e: [CR[t, e], ZB[v, e - 2]])
            z_hop(v, 3).start()

    def finish_down(v):
        z_hop(v, 2).wait_recv()
        z_hop(v, 3).wait_recv()
        for lo in (0, 2):
            core_wait(6 + v, lo)
            add_blocks(6 + v, lo, lambda e: [CR[6 + v, e], ZC[v, e], ZD[v, e]], into=v)

    comb_own = pltpu.make_async_copy(comb_hbm, META.at[me, pl.ds(0, 8)], misc_s.at[0])
    route_own = pltpu.make_async_copy(route_hbm, ROUTE, misc_s.at[4])
    comb_own.start()
    route_own.start()
    for t in range(TICKS):
        for h in range(2):
            own_copy(t, h).start()
    hid_copy = pltpu.make_async_copy(hid_hbm, H, misc_s.at[1])
    in_copy = pltpu.make_async_copy(in_hbm, INP, misc_s.at[2])
    rw_copy = pltpu.make_async_copy(rw_hbm, RW, misc_s.at[3])
    inc_own = pltpu.make_async_copy(
        in_hbm.at[:, pl.ds(pl.multiple_of(me * LANE, LANE), LANE)], INC.at[me], misc_s.at[5]
    )

    barrier = pltpu.get_barrier_semaphore()
    @pl.loop(1, NE)
    def _(d):
        pl.semaphore_signal(barrier, inc=1, device_id=expert_dev(lax.rem(me + d, NE)),
                            device_id_type=pl.DeviceIdType.MESH)
    @pl.loop(1, NDP)
    def _(d):
        pl.semaphore_signal(barrier, inc=1, device_id=dp_dev(lax.rem(dp + d, NDP)),
                            device_id_type=pl.DeviceIdType.MESH)
    hid_copy.start()
    comb_own.wait()
    route_own.wait()
    META[me, 8:16, :] = ROUTE[...].astype(F32)
    pl.semaphore_wait(barrier, NE - 1 + NDP - 1)

    def plane_to(d):
        return expert_dev(lax.rem(me + d, NE))

    def plane_from(d):
        return lax.rem(me + NE - d, NE)

    def meta_send(d):
        return remote(META.at[me], META.at[me], meta_s.at[d], meta_r.at[d], plane_to(d))

    def meta_recv(d):
        got = META.at[plane_from(d)]
        return remote(got, got, meta_s.at[d], meta_r.at[d], plane_to(d))

    def inc_send(d):
        cols = pl.ds(pl.multiple_of(lax.rem(me + d, NE) * LANE, LANE), LANE)
        return remote(INP.at[:, cols], INC.at[me], inc_s.at[d], inc_r.at[d], plane_to(d))

    def inc_recv(d):
        got = INC.at[plane_from(d)]
        return remote(got, got, inc_s.at[d], inc_r.at[d], plane_to(d))

    def build_gates(src):
        block = META[src]
        expert_id = lax.broadcasted_iota(jnp.int32, (NE * n_exp, LANE), 0).astype(F32)
        gate = jnp.zeros((NE * n_exp, LANE), F32)
        for k in range(8):
            gate += jnp.where(expert_id == block[8 + k:9 + k], block[k:k + 1], 0.0)
        GATE[src] = gate

    def build_codes():
        @pl.loop(1, NE)
        def _(d):
            meta_recv(d).wait_recv()

        @pl.loop(0, NE // 2)
        def _(p):
            marks, gains = [], []
            for s2 in range(2):
                block = META[2 * p + s2]
                cb, rt = block[0:8], block[8:16]
                for e in range(n_exp):
                    hit = rt == (me * n_exp + e).astype(F32)
                    marks.append(jnp.sum(jnp.where(hit, 1.0, 0.0), axis=0, keepdims=True))
                    gains.append(jnp.sum(jnp.where(hit, cb, 0.0), axis=0, keepdims=True))
            at = pl.ds(pl.multiple_of(8 * p, 8), 8)
            CODES[at, :] = jnp.concatenate(marks, axis=0)
            GROW[at, :] = jnp.concatenate(gains, axis=0)

        marks = CODES[...]
        r = lax.broadcasted_iota(jnp.int32, (LANE, LANE), 0)
        q = lax.broadcasted_iota(jnp.int32, (LANE, LANE), 1)
        earlier = jnp.where(r < q, 1.0, 0.0).astype(BF)
        before = jnp.dot(marks.astype(BF), earlier, preferred_element_type=F32)
        CODES[...] = jnp.where(marks > 0.5, before, -1000.0)

    def build_dispatch():
        place = lax.broadcasted_iota(jnp.int32, (pair, LANE), 0).astype(F32)
        @pl.loop(0, NE // 2)
        def _(p):
            at = pl.ds(pl.multiple_of(8 * p, 8), 8)
            codes = CODES[at, :]
            gains = GROW[at, :]
            for e in range(n_exp):
                first = jnp.where(place == codes[e:e + 1], 1.0, 0.0)
                second = jnp.where(place - cap == codes[n_exp + e:n_exp + e + 1], 1.0, 0.0)
                S[p, e * pair:(e + 1) * pair, 0:LANE] = first.astype(BF)
                S[p, e * pair:(e + 1) * pair, LANE:2 * LANE] = second.astype(BF)
                gain = jnp.sum(
                    first * gains[e:e + 1] + second * gains[n_exp + e:n_exp + e + 1],
                    axis=1, keepdims=True,
                )
                GAIN[p, e * pair:(e + 1) * pair, :] = jnp.broadcast_to(gain, (pair, LANE))

    def compute(t):
        for h in range(2):
            w_copy(t, h).wait()
        for p in range(NE // 2):
            yy, xx = p // 2, 2 * (p % 2)
            g0 = G[t, 0, yy, xx:xx + 2].reshape(2 * LANE, LANE)
            g1 = G[t, 1, yy, xx:xx + 2].reshape(2 * LANE, LANE)
            rows = jnp.dot(S[p], jnp.concatenate([g0, g1], axis=1), preferred_element_type=F32)
            gain = GAIN[p]
            rows = (rows * jnp.concatenate([gain, gain], axis=1)).astype(BF)
            for e in range(n_exp):
                X[e, p * pair:(p + 1) * pair, :] = rows[e * pair:(e + 1) * pair]

        @pl.loop(0, n_exp)
        def _(e):
            xe = X[e]
            we = W[t, e].reshape(2 * LANE, width_ff)
            HG[e] += jnp.dot(xe, we, preferred_element_type=F32)
            grad = lax.dot_general(xe, H[e], (((0,), (0,)), ((), ())), preferred_element_type=F32)

            @pl.when(t >= 2)
            def _():
                core_hop(t - 2, e).wait_send()

            CS[lax.rem(t, 2), e] = grad[:LANE].astype(BF)
            core_hop(t, e).start()
            OWN[t, e] = grad[LANE:].astype(BF)

            @pl.when(e == 0)
            def _():
                gather_ahead(t)

    def phase_start(t, phase):
        for h in range(2):
            if phase == 0:
                own_copy(t, h).wait()
            hop_start(t, h, 2 * phase)
            hop_start(t, h, 2 * phase + 1)

    def phase_wait(t, phase):
        for h in range(2):
            hop_wait(t, h, 2 * phase)
            hop_wait(t, h, 2 * phase + 1)

    def gather_ahead(t):
        @pl.when(t + 1 < TICKS)
        def _():
            phase_wait(t + 1, 2)
            phase_start(t + 1, 3)

        @pl.when(t + 3 < TICKS)
        def _():
            phase_wait(t + 3, 1)
            phase_start(t + 3, 2)

        @pl.when(t + 5 < TICKS)
        def _():
            phase_wait(t + 5, 0)
            phase_start(t + 5, 1)

        @pl.when(t + 7 < TICKS)
        def _():
            phase_start(t + 7, 0)

        @pl.when(t + 2 == TICKS)
        def _():
            in_copy.wait()
            @pl.loop(1, NE)
            def _(d):
                inc_send(d).start()

    phase_start(0, 0)
    phase_start(1, 0)
    @pl.loop(1, NE)
    def _(d):
        meta_send(d).start()
    phase_wait(0, 0)
    phase_start(0, 1)
    phase_start(2, 0)
    phase_wait(0, 1)
    phase_start(0, 2)
    for t in range(TICKS):
        for h in range(2):
            w_copy(t, h).start()
    in_copy.start()
    rw_copy.start()
    inc_own.start()
    phase_wait(1, 0)
    phase_start(1, 1)
    phase_start(3, 0)
    HG[...] = jnp.zeros_like(HG)
    build_codes()
    phase_wait(2, 0)
    phase_start(2, 1)
    phase_start(4, 0)
    phase_wait(0, 2)
    phase_start(0, 3)
    phase_wait(1, 1)
    phase_start(1, 2)
    phase_start(5, 0)
    phase_wait(3, 0)
    phase_start(3, 1)
    build_dispatch()
    phase_wait(2, 1)
    phase_start(2, 2)
    phase_wait(4, 0)
    phase_start(4, 1)
    phase_start(6, 0)
    hid_copy.wait()

    @pl.loop(0, TICKS)
    def _(t):
        phase_wait(t, 3)
        compute(t)

        @pl.when(t < 6)
        def _():
            pair_up(t)

        build_gates(2 * t)
        build_gates(2 * t + 1)

    for e in range(n_exp):
        hg = HG[e]
        hg_out[e] = hg.astype(BF)
        prod = jnp.sum(H[e].astype(F32) * hg, axis=1, keepdims=True)
        for p in range(NE // 2):
            row = jnp.sum(
                S[p, e * pair:(e + 1) * pair, :].astype(F32) * prod[p * pair:(p + 1) * pair],
                axis=0, keepdims=True,
            )
            at = n_exp * (p // 2) + e
            PROD[at:at + 1, (p % 2) * 256:(p % 2) * 256 + 256] = row
    PSB[me] = PROD[...].astype(BF)

    def ps_send(d):
        return remote(PSB.at[me], PSB.at[me], ps_s.at[d], ps_r.at[d], plane_to(d))

    def ps_recv(d):
        got = PSB.at[plane_from(d)]
        return remote(got, got, ps_s.at[d], ps_r.at[d], plane_to(d))

    @pl.loop(1, NE)
    def _(d):
        ps_send(d).start()
    inc_own.wait()
    rw_copy.wait()

    @pl.loop(0, TICKS)
    def _(t):
        for h in range(2):
            for k in range(8):
                hop_drain(t, h, k)

    @pl.loop(1, NE)
    def _(d):
        inc_recv(d).wait_recv()
    @pl.loop(1, NE)
    def _(d):
        ps_recv(d).wait_recv()

    for i in range(NE // 2):
        low, high = PSB[2 * i].astype(F32), PSB[2 * i + 1].astype(F32)
        for g in range(4):
            rows = slice(n_exp * g, n_exp * (g + 1))
            SUMS[8 * i:8 * i + 8, g * 512:(g + 1) * 512] = jnp.concatenate(
                [low[rows], high[rows]], axis=0
            )
    acc = jnp.zeros((NE * n_exp, LANE), F32)
    for q in range(NE // 2):
        both = []
        for src in (2 * q, 2 * q + 1):
            sums = SUMS[:, src * LANE:(src + 1) * LANE]
            total = jnp.sum(sums, axis=0, keepdims=True)
            dense = (sums - GATE[src] * total).astype(BF)
            DENSE[src] = dense
            both.append(dense)
        acc += jnp.dot(
            jnp.concatenate(both, axis=1), INC[2 * q:2 * q + 2].reshape(2 * LANE, LANE),
            preferred_element_type=F32,
        )
    rows_half = NE * n_exp // 2
    PF[0] = acc[:rows_half]
    PF[1] = acc[rows_half:]

    other = dp_dev(2 * z + 1 - c)

    def r2_send(d):
        to = lax.rem(dp + d, NDP)
        return remote(PF.at[lax.rem(to, 2)], R2.at[dp], r2_s.at[d], r2_r.at[d], dp_dev(to))

    def r2_recv(d):
        got = R2.at[lax.rem(dp + NDP - d, NDP)]
        return remote(got, got, r2_s.at[d], r2_r.at[d], dp_dev(lax.rem(dp + d, NDP)))

    def r3_send(d):
        return remote(OUT.at[c, me], OUT.at[c, me], r3_s.at[d], r3_r.at[d], plane_to(d))

    def r3_recv(d):
        got = OUT.at[c, plane_from(d)]
        return remote(got, got, r3_s.at[d], r3_r.at[d], plane_to(d))

    def r4_send():
        return remote(OUT.at[c], OUT.at[c], r4_s, r4_r, other)

    def r4_recv():
        return remote(OUT.at[1 - c], OUT.at[1 - c], r4_s, r4_r, other)

    @pl.loop(1, NDP)
    def _(d):
        r2_send(d).start()
    R2[dp] = PF[c]
    own_dense = DENSE[me]
    for q in range(4):
        cols = slice(q * 512, (q + 1) * 512)
        ig_out[:, cols] = lax.dot_general(
            own_dense, RW[:, cols], (((0,), (0,)), ((), ())), preferred_element_type=F32
        ).astype(BF)
    @pl.loop(1, NDP)
    def _(d):
        r2_recv(d).wait_recv()
    acc = R2[0]
    for j in range(1, NDP):
        acc += R2[j]
    OUT[c, me] = acc
    @pl.loop(1, NE)
    def _(d):
        r3_send(d).start()
    finish_down(0)
    @pl.loop(1, NE)
    def _(d):
        meta_send(d).wait_send()
        inc_send(d).wait_send()
        ps_send(d).wait_send()
    @pl.loop(1, NDP)
    def _(d):
        r2_send(d).wait_send()
    for e in range(n_exp):
        core_hop(TICKS - 2, e).wait_send()
        core_hop(TICKS - 1, e).wait_send()
    for k in range(4):
        z_hop(0, k).wait_send()
    for k in range(2):
        z_hop(1, k).wait_send()
    @pl.loop(1, NE)
    def _(d):
        r3_recv(d).wait_recv()
    r4_send().start()
    finish_down(1)
    @pl.loop(1, NE)
    def _(d):
        r3_send(d).wait_send()
    r4_recv().wait_recv()
    for j in range(NE):
        for half in range(2):
            rp_out[half * rows_half:(half + 1) * rows_half, j * LANE:(j + 1) * LANE] = OUT[half, j]

    r4_send().wait_send()
    for k in (2, 3):
        z_hop(1, k).wait_send()


def local(inputs, out_grad, combine, routes, saved_hidden, down_weight, router_weight):
    tokens, width = out_grad.shape
    n_exp, _, ff = down_weight.shape
    total = router_weight.shape[0]
    slots = saved_hidden.shape[2] * saved_hidden.shape[3]
    pair = slots // (NE // 2)
    hidden = saved_hidden.reshape(n_exp, slots, ff)
    dma = pltpu.SemaphoreType.DMA
    hg, dw, ig, rp = pl.pallas_call(
        fused,
        out_shape=(
            pltpu.VMEM((n_exp, slots, ff), BF),
            pltpu.VMEM((n_exp, width // NDP, ff), BF),
            pltpu.VMEM((tokens, width), BF),
            pltpu.VMEM((total, width), F32),
        ),
        in_specs=[pl.BlockSpec(memory_space=pl.ANY)] * 7,
        out_specs=(pl.BlockSpec(memory_space=pltpu.VMEM),) * 4,
        scratch_shapes=[
            pltpu.VMEM((TICKS, 2, NY, NX, tokens, LANE), BF),
            pltpu.VMEM((TICKS, n_exp, 2, LANE, ff), BF),
            pltpu.VMEM((n_exp, slots, ff), BF),
            pltpu.VMEM((n_exp, slots, ff), F32),
            pltpu.VMEM((n_exp, slots, 2 * LANE), BF),
            pltpu.VMEM((NE // 2, n_exp * pair, 2 * LANE), BF),
            pltpu.VMEM((NE // 2, n_exp * pair, LANE), F32),
            pltpu.VMEM((NE, 16, LANE), F32),
            pltpu.VMEM((8, LANE), jnp.int32),
            pltpu.VMEM((NE * n_exp, LANE), F32),
            pltpu.VMEM((NE * n_exp, LANE), F32),
            pltpu.VMEM((2, n_exp, LANE, ff), BF),
            pltpu.VMEM((TICKS, n_exp, LANE, ff), BF),
            pltpu.VMEM((TICKS, n_exp, LANE, ff), BF),
            pltpu.VMEM((2, 2, LANE, ff), BF),
            pltpu.VMEM((2, 2, LANE, ff), BF),
            pltpu.VMEM((2, n_exp, LANE, ff), BF),
            pltpu.VMEM((2, n_exp, LANE, ff), BF),
            pltpu.VMEM((tokens, width), BF),
            pltpu.VMEM((NE, tokens, LANE), BF),
            pltpu.VMEM((total, width), BF),
            pltpu.VMEM((NE, total, LANE), F32),
            pltpu.VMEM((16, 512), F32),
            pltpu.VMEM((NE, 16, 512), BF),
            pltpu.VMEM((total, NE * tokens), F32),
            pltpu.VMEM((NE, total, LANE), BF),
            pltpu.VMEM((2, total // 2, LANE), F32),
            pltpu.VMEM((NDP, total // 2, LANE), F32),
            pltpu.VMEM((2, NE, total // 2, LANE), F32),
            dma((TICKS, 2, 8)),
            dma((TICKS, 2, 8)),
            dma((TICKS, 2)),
            dma((TICKS, 2)),
            dma((6,)),
            dma((NE,)),
            dma((NE,)),
            dma((TICKS, n_exp)),
            dma((TICKS, n_exp)),
            dma((2, 4)),
            dma((2, 4)),
            dma((NE,)),
            dma((NE,)),
            dma((NE,)),
            dma((NE,)),
            dma((NDP,)),
            dma((NDP,)),
            dma((NE,)),
            dma((NE,)),
            dma,
            dma,
        ],
        compiler_params=pltpu.CompilerParams(
            collective_id=0, has_side_effects=True, vmem_limit_bytes=58 * 2**20
        ),
        name="moe_down_backward",
    )(combine.T, routes.T, out_grad, hidden, down_weight, inputs, router_weight)
    return hg.reshape(saved_hidden.shape), dw, ig, rp


def solution(mesh):
    placed = (
        P(("dp", "expert"), None),
        P(("dp", "expert"), None),
        P(("dp", "expert"), None),
        P(("dp", "expert"), None),
        P("dp", "expert", None, None, None),
        P("expert", None, None),
        P(),
    )
    return jax.shard_map(
        local,
        mesh=mesh,
        in_specs=placed,
        out_specs=(
            P("dp", "expert", None, None, None),
            P("expert", "dp", None),
            P(("dp", "expert"), None),
            P(),
        ),
        check_vma=False,
    )
```

```python
import jax
import jax.numpy as jnp
from jax import lax
from jax.experimental import pallas as pl
from jax.experimental.pallas import tpu as pltpu
from jax.sharding import PartitionSpec as P

NX = 4
NY = 4
NZ = 4
NE = NX * NY
NDP = 2 * NZ
TICKS = 8
LANE = 128
BF = jnp.bfloat16
F32 = jnp.float32


def remote(src, dst, ssem, rsem, dev):
    return pltpu.make_async_remote_copy(
        src_ref=src, dst_ref=dst, send_sem=ssem, recv_sem=rsem,
        device_id=dev, device_id_type=pl.DeviceIdType.MESH,
    )


def fused(
    comb_hbm, route_hbm, og_hbm, hid_hbm, w_hbm, in_hbm, rw_hbm,
    hg_out, dw_out, ig_out, rp_out,
    G, W, H, HG, X, S, GAIN, META, ROUTE, CODES, GROW, RR, RSEND, RRECV,
    CS, CR, OWN, ZA, ZB, ZC, ZD, INP, RW, IG, RP, RC, R1, R2, OUT,
    ag_s, ag_r, own_s, w_s, misc_s, hg_s, out_s, meta_s, meta_r, ret_s, ret_r,
    core_s, core_r, z_s, z_r, r1_s, r1_r, r2_s, r2_r, r3_s, r3_r, rc_s, rc_r, rp_s,
):
    n_exp, slots, width_ff = hid_hbm.shape
    cap = slots // NE
    pair = 2 * cap
    me = lax.axis_index("expert")
    dp = lax.axis_index("dp")
    y, x = me // NX, lax.rem(me, NX)
    z, c = dp // 2, lax.rem(dp, 2)

    def expert_dev(index):
        return {"expert": index}

    def column(t, h):
        step = jnp.where(t < 2, 2, jnp.where(t >= 6, 0, 1 + 2 * lax.rem(t, 2)))
        v = jnp.where(t < 2, t, jnp.where(t >= 6, t - 6, (t - 2) // 2))
        zz = lax.rem(z + step, NZ)
        core = 1 - c if h == 0 else c
        return pl.multiple_of((2 * zz + core) * 256 + v * LANE, LANE)

    def axes(h):
        return (x, y) if h == 0 else (y, x)

    def cell(t, h, a, b):
        return G.at[t, h, b, a] if h == 0 else G.at[t, h, a, b]

    def dev(h, a, b):
        return expert_dev(b * NX + a) if h == 0 else expert_dev(a * NX + b)

    def line(t, h, b, lo, n):
        return G.at[t, h, b, pl.ds(lo, n)] if h == 0 else G.at[t, h, pl.ds(lo, n), b]

    def up(i):
        return lax.rem(i + 1, 4)

    def down(i):
        return lax.rem(i + 3, 4)

    def far(i):
        return lax.rem(i + 2, 4)

    def hop(t, h, k):
        a, b = axes(h)
        if k == 0:
            return cell(t, h, a, b), cell(t, h, down(a), b), dev(h, up(a), b)
        if k == 1:
            return cell(t, h, a, b), cell(t, h, up(a), b), dev(h, down(a), b)
        if k == 2:
            lo = pl.ds(0, 64)
            return cell(t, h, down(a), b).at[lo], cell(t, h, far(a), b).at[lo], dev(h, up(a), b)
        if k == 3:
            hi = pl.ds(64, 64)
            return cell(t, h, up(a), b).at[hi], cell(t, h, far(a), b).at[hi], dev(h, down(a), b)
        if k == 4:
            return line(t, h, b, 0, 4), line(t, h, down(b), 0, 4), dev(h, a, up(b))
        if k == 5:
            return line(t, h, b, 0, 4), line(t, h, up(b), 0, 4), dev(h, a, down(b))
        if k == 6:
            return line(t, h, down(b), 0, 2), line(t, h, far(b), 0, 2), dev(h, a, up(b))
        return line(t, h, up(b), 2, 2), line(t, h, far(b), 2, 2), dev(h, a, down(b))

    def hop_start(t, h, k):
        sent, _, to = hop(t, h, k)
        remote(sent, sent, ag_s.at[t, h, k], ag_r.at[t, h, k], to).start()

    def hop_wait(t, h, k):
        _, got, to = hop(t, h, k)
        remote(got, got, ag_s.at[t, h, k], ag_r.at[t, h, k], to).wait_recv()

    def hop_drain(t, h, k):
        sent, _, to = hop(t, h, k)
        remote(sent, sent, ag_s.at[t, h, k], ag_r.at[t, h, k], to).wait_send()

    def own_copy(t, h):
        a, b = axes(h)
        return pltpu.make_async_copy(
            og_hbm.at[:, pl.ds(column(t, h), LANE)], cell(t, h, a, b), own_s.at[t, h]
        )

    def w_copy(t, h):
        return pltpu.make_async_copy(
            w_hbm.at[:, pl.ds(column(t, h), LANE), :], W.at[t, :, h], w_s.at[t, h]
        )

    def dp_dev(index):
        return {"dp": index}

    next_z = dp_dev(2 * lax.rem(z + 1, NZ) + c)
    prev_z = dp_dev(2 * lax.rem(z + 3, NZ) + c)

    def core_hop(t, e):
        return remote(
            CS.at[lax.rem(t, 2), e], CR.at[t, e], core_s.at[t, e], core_r.at[t, e],
            dp_dev(2 * z + 1 - c),
        )

    def z_hop(v, k):
        t = v if k < 2 else k + 2 * v
        if k == 0:
            sent, land = OWN.at[t, pl.ds(0, 2)], ZA.at[v]
        elif k == 1:
            sent, land = OWN.at[t, pl.ds(2, 2)], ZB.at[v]
        else:
            sent, land = OWN.at[t], (ZC.at[v] if k == 2 else ZD.at[v])
        return remote(sent, land, z_s.at[v, k], z_r.at[v, k], next_z if k in (0, 2) else prev_z)

    def add_blocks(t, lo, others):
        for e in range(lo, lo + 2):
            acc = OWN[t, e].astype(F32)
            for other in others(e):
                acc += other.astype(F32)
            OWN[t, e] = acc.astype(BF)

    def core_wait(t, lo):
        for e in (lo, lo + 1):
            core_hop(t, e).wait_recv()

    def pair_up(t):
        @pl.when(t < 2)
        def _():
            for k in range(2):
                core_wait(t, 2 * k)
                add_blocks(t, 2 * k, lambda e: [CR[t, e]])
                z_hop(t, k).start()

        @pl.when((t == 2) | (t == 4))
        def _():
            v = (t - 2) // 2
            z_hop(v, 0).wait_recv()
            core_wait(t, 0)
            add_blocks(t, 0, lambda e: [CR[t, e], ZA[v, e]])
            core_wait(t, 2)
            add_blocks(t, 2, lambda e: [CR[t, e]])
            z_hop(v, 2).start()

        @pl.when((t == 3) | (t == 5))
        def _():
            v = (t - 2) // 2
            core_wait(t, 0)
            add_blocks(t, 0, lambda e: [CR[t, e]])
            z_hop(v, 1).wait_recv()
            core_wait(t, 2)
            add_blocks(t, 2, lambda e: [CR[t, e], ZB[v, e - 2]])
            z_hop(v, 3).start()

    def dw_copy(v):
        return pltpu.make_async_copy(
            OWN.at[6 + v], dw_out.at[:, pl.ds(v * LANE, LANE), :], out_s.at[2 + v]
        )

    def finish_down(v):
        z_hop(v, 2).wait_recv()
        z_hop(v, 3).wait_recv()
        for lo in (0, 2):
            core_wait(6 + v, lo)
            add_blocks(6 + v, lo, lambda e: [CR[6 + v, e], ZC[v, e], ZD[v, e]])
        dw_copy(v).start()

    comb_own = pltpu.make_async_copy(comb_hbm, META.at[me, pl.ds(0, 8)], misc_s.at[0])
    route_own = pltpu.make_async_copy(route_hbm, ROUTE, misc_s.at[4])
    comb_own.start()
    route_own.start()
    for t in range(TICKS):
        for h in range(2):
            own_copy(t, h).start()
    hid_copy = pltpu.make_async_copy(hid_hbm, H, misc_s.at[1])
    in_copy = pltpu.make_async_copy(in_hbm, INP, misc_s.at[2])
    rw_copy = pltpu.make_async_copy(rw_hbm, RW, misc_s.at[3])

    barrier = pltpu.get_barrier_semaphore()
    for d in range(1, NE):
        pl.semaphore_signal(barrier, inc=1, device_id=expert_dev(lax.rem(me + d, NE)),
                            device_id_type=pl.DeviceIdType.MESH)
    for d in range(1, NDP):
        pl.semaphore_signal(barrier, inc=1, device_id=dp_dev(lax.rem(dp + d, NDP)),
                            device_id_type=pl.DeviceIdType.MESH)
    hid_copy.start()
    comb_own.wait()
    route_own.wait()
    META[me, 8:16, :] = ROUTE[...].astype(F32)
    pl.semaphore_wait(barrier, NE - 1 + NDP - 1)

    def plane_to(d):
        return expert_dev(lax.rem(me + d, NE))

    def plane_from(d):
        return lax.rem(me + NE - d, NE)

    def meta_send(d):
        return remote(META.at[me], META.at[me], meta_s.at[d], meta_r.at[d], plane_to(d))

    def meta_recv(d):
        got = META.at[plane_from(d)]
        return remote(got, got, meta_s.at[d], meta_r.at[d], plane_to(d))

    def build_codes():
        for d in range(1, NE):
            meta_recv(d).wait_recv()

        for p in range(NE // 2):
            marks, gains = [], []
            for s2 in range(2):
                block = META[2 * p + s2]
                cb, rt = block[0:8], block[8:16]
                for e in range(n_exp):
                    hit = rt == (me * n_exp + e).astype(F32)
                    marks.append(jnp.sum(jnp.where(hit, 1.0, 0.0), axis=0, keepdims=True))
                    gains.append(jnp.sum(jnp.where(hit, cb, 0.0), axis=0, keepdims=True))
            CODES[8 * p:8 * p + 8, :] = jnp.concatenate(marks, axis=0)
            GROW[8 * p:8 * p + 8, :] = jnp.concatenate(gains, axis=0)

        marks = CODES[...]
        r = lax.broadcasted_iota(jnp.int32, (LANE, LANE), 0)
        q = lax.broadcasted_iota(jnp.int32, (LANE, LANE), 1)
        earlier = jnp.where(r < q, 1.0, 0.0).astype(BF)
        before = jnp.dot(marks.astype(BF), earlier, preferred_element_type=F32)
        CODES[...] = jnp.where(marks > 0.5, before, -1000.0)

    def build_dispatch():
        place = lax.broadcasted_iota(jnp.int32, (pair, LANE), 0).astype(F32)
        for p in range(NE // 2):
            codes = CODES[8 * p:8 * p + 8, :]
            gains = GROW[8 * p:8 * p + 8, :]
            for e in range(n_exp):
                first = jnp.where(place == codes[e:e + 1], 1.0, 0.0)
                second = jnp.where(place - cap == codes[n_exp + e:n_exp + e + 1], 1.0, 0.0)
                S[p, e * pair:(e + 1) * pair, 0:LANE] = first.astype(BF)
                S[p, e * pair:(e + 1) * pair, LANE:2 * LANE] = second.astype(BF)
                gain = jnp.sum(
                    first * gains[e:e + 1] + second * gains[n_exp + e:n_exp + e + 1],
                    axis=1, keepdims=True,
                )
                GAIN[p, e * pair:(e + 1) * pair, :] = jnp.broadcast_to(gain, (pair, LANE))

    def compute(t):
        for h in range(2):
            w_copy(t, h).wait()
        for p in range(NE // 2):
            yy, xx = p // 2, 2 * (p % 2)
            g0 = G[t, 0, yy, xx:xx + 2].reshape(2 * LANE, LANE)
            g1 = G[t, 1, yy, xx:xx + 2].reshape(2 * LANE, LANE)
            rows = jnp.dot(S[p], jnp.concatenate([g0, g1], axis=1), preferred_element_type=F32)
            gain = GAIN[p]
            rows = (rows * jnp.concatenate([gain, gain], axis=1)).astype(BF)
            for e in range(n_exp):
                X[e, p * pair:(p + 1) * pair, :] = rows[e * pair:(e + 1) * pair]

        @pl.loop(0, n_exp)
        def _(e):
            xe = X[e]
            we = W[t, e].reshape(2 * LANE, width_ff)
            HG[e] += jnp.dot(xe, we, preferred_element_type=F32)
            grad = lax.dot_general(xe, H[e], (((0,), (0,)), ((), ())), preferred_element_type=F32)

            @pl.when(t >= 2)
            def _():
                core_hop(t - 2, e).wait_send()

            CS[lax.rem(t, 2), e] = grad[:LANE].astype(BF)
            core_hop(t, e).start()
            OWN[t, e] = grad[LANE:].astype(BF)

            @pl.when(e == 0)
            def _():
                gather_ahead(t)

    def phase_start(t, phase):
        for h in range(2):
            if phase == 0:
                own_copy(t, h).wait()
            hop_start(t, h, 2 * phase)
            hop_start(t, h, 2 * phase + 1)

    def phase_wait(t, phase):
        for h in range(2):
            hop_wait(t, h, 2 * phase)
            hop_wait(t, h, 2 * phase + 1)

    def gather_ahead(t):
        @pl.when(t + 1 < TICKS)
        def _():
            phase_wait(t + 1, 2)
            phase_start(t + 1, 3)

        @pl.when(t + 3 < TICKS)
        def _():
            phase_wait(t + 3, 1)
            phase_start(t + 3, 2)

        @pl.when(t + 5 < TICKS)
        def _():
            phase_wait(t + 5, 0)
            phase_start(t + 5, 1)

        @pl.when(t + 7 < TICKS)
        def _():
            phase_start(t + 7, 0)

    phase_start(0, 0)
    phase_start(1, 0)
    for d in range(1, NE):
        meta_send(d).start()
    phase_wait(0, 0)
    phase_start(0, 1)
    phase_start(2, 0)
    phase_wait(0, 1)
    phase_start(0, 2)
    for t in range(TICKS):
        for h in range(2):
            w_copy(t, h).start()
    in_copy.start()
    rw_copy.start()
    phase_wait(1, 0)
    phase_start(1, 1)
    phase_start(3, 0)
    HG[...] = jnp.zeros_like(HG)
    build_codes()
    phase_wait(2, 0)
    phase_start(2, 1)
    phase_start(4, 0)
    phase_wait(0, 2)
    phase_start(0, 3)
    phase_wait(1, 1)
    phase_start(1, 2)
    phase_start(5, 0)
    phase_wait(3, 0)
    phase_start(3, 1)
    build_dispatch()
    phase_wait(2, 1)
    phase_start(2, 2)
    phase_wait(4, 0)
    phase_start(4, 1)
    phase_start(6, 0)
    hid_copy.wait()

    @pl.loop(0, TICKS)
    def _(t):
        phase_wait(t, 3)
        compute(t)

        @pl.when(t < 6)
        def _():
            pair_up(t)

    for e in range(n_exp):
        hg = HG[e]
        for q in range(3):
            W[e, q // 2, q % 2] = hg[q * LANE:(q + 1) * LANE].astype(BF)
        prod = jnp.sum(H[e].astype(F32) * hg, axis=1, keepdims=True)
        for p in range(NE // 2):
            row = jnp.sum(
                S[p, e * pair:(e + 1) * pair, :].astype(F32) * prod[p * pair:(p + 1) * pair],
                axis=0, keepdims=True,
            )
            RR[p, e:e + 1, :] = row
            RR[p, n_exp + e:n_exp + e + 1, :] = row
    half = lax.broadcasted_iota(jnp.int32, (8, LANE), 0) // n_exp
    mine = half == lax.rem(me, 2)
    for p in range(NE // 2):
        for s2 in range(2):
            RSEND[2 * p + s2] = jnp.where(mine, RR[p, :, s2 * LANE:(s2 + 1) * LANE], 0.0)

    def ret_send(d):
        out = RSEND.at[lax.rem(me + d, NE)]
        return remote(out, RRECV.at[me], ret_s.at[d], ret_r.at[d], plane_to(d))

    def ret_recv(d):
        got = RRECV.at[plane_from(d)]
        return remote(got, got, ret_s.at[d], ret_r.at[d], plane_to(d))

    for d in range(1, NE):
        ret_send(d).start()
    RRECV[me] = RSEND[me]

    def hg_copy(e, q):
        return pltpu.make_async_copy(
            W.at[e, q // 2, q % 2], hg_out.at[e, pl.ds(q * LANE, LANE)], hg_s.at[e, q]
        )

    for e in range(n_exp):
        for q in range(3):
            hg_copy(e, q).start()

    own_meta = META[me]
    expert_id = lax.broadcasted_iota(jnp.int32, (NE * n_exp, LANE), 0).astype(F32)
    gate = jnp.zeros((NE * n_exp, LANE), F32)
    named = jnp.zeros((NE * n_exp, LANE), F32)
    for k in range(8):
        hit = expert_id == own_meta[8 + k:9 + k]
        gate += jnp.where(hit, own_meta[k:k + 1], 0.0)
        named += jnp.where(hit, 1.0, 0.0)

    in_copy.wait()
    rw_copy.wait()
    @pl.loop(0, TICKS)
    def _(t):
        for h in range(2):
            for k in range(8):
                hop_drain(t, h, k)

    for d in range(1, NE):
        ret_recv(d).wait_recv()
    sums = jnp.concatenate([RRECV[2 * q] + RRECV[2 * q + 1] for q in range(NE // 2)], axis=0)
    total = jnp.sum(sums, axis=0, keepdims=True)
    dense = jnp.where(named > 0.5, sums - gate * total, 0.0).astype(BF)
    rows_half = NE * n_exp // 2
    for q in range(4):
        cols = slice(q * 512, (q + 1) * 512)
        part = jnp.dot(dense, INP[:, cols], preferred_element_type=F32)
        for j in range(4):
            block = part[:, j * LANE:(j + 1) * LANE]
            RP[4 * q + j, 0] = block[:rows_half]
            RP[4 * q + j, 1] = block[rows_half:]

    other = dp_dev(2 * z + 1 - c)

    def rc_send():
        return remote(RP.at[:, 1 - c], RC, rc_s.at[0], rc_r.at[0], other)

    def r1_send(d):
        out = RP.at[lax.rem(me + d, NE), c]
        return remote(out, R1.at[me], r1_s.at[d], r1_r.at[d], plane_to(d))

    def r1_recv(d):
        got = R1.at[plane_from(d)]
        return remote(got, got, r1_s.at[d], r1_r.at[d], plane_to(d))

    def r2_send(d):
        to = dp_dev(2 * lax.rem(z + d, NZ) + c)
        return remote(R2.at[z], R2.at[z], r2_s.at[d], r2_r.at[d], to)

    def r2_recv(d):
        got = R2.at[lax.rem(z + NZ - d, NZ)]
        return remote(got, got, r2_s.at[d], r2_r.at[d], dp_dev(2 * lax.rem(z + d, NZ) + c))

    def r3_send(d):
        return remote(OUT.at[me, c], OUT.at[me, c], r3_s.at[d], r3_r.at[d], plane_to(d))

    def r3_recv(d):
        got = OUT.at[plane_from(d), c]
        return remote(got, got, r3_s.at[d], r3_r.at[d], plane_to(d))

    def r4_send():
        return remote(OUT.at[:, c], OUT.at[:, c], rc_s.at[1], rc_r.at[1], other)

    def r4_recv():
        return remote(OUT.at[:, 1 - c], OUT.at[:, 1 - c], rc_s.at[1], rc_r.at[1], other)

    rc_send().start()
    rc_send().wait_recv()
    for j in range(NE):
        RP[j, c] += RC[j]
    for d in range(1, NE):
        r1_send(d).start()
    R1[me] = RP[me, c]
    for q in range(4):
        cols = slice(q * 512, (q + 1) * 512)
        IG[:, cols] = lax.dot_general(
            dense, RW[:, cols], (((0,), (0,)), ((), ())), preferred_element_type=F32
        ).astype(BF)
    ig_copy = pltpu.make_async_copy(IG, ig_out, out_s.at[0])
    ig_copy.start()

    for d in range(1, NE):
        r1_recv(d).wait_recv()
    acc = R1[0]
    for j in range(1, NE):
        acc += R1[j]
    R2[z] = acc
    for d in range(1, NZ):
        r2_send(d).start()
    finish_down(0)
    for d in range(1, NZ):
        r2_recv(d).wait_recv()
    acc = R2[0]
    for j in range(1, NZ):
        acc += R2[j]
    OUT[me, c] = acc
    for d in range(1, NE):
        r3_send(d).start()
    finish_down(1)
    for d in range(1, NE):
        r3_recv(d).wait_recv()
    r4_send().start()
    r4_recv().wait_recv()

    def rp_copy(j, half):
        return pltpu.make_async_copy(
            OUT.at[j, half],
            rp_out.at[pl.ds(half * rows_half, rows_half), pl.ds(j * LANE, LANE)],
            rp_s.at[j, half],
        )

    for j in range(NE):
        rp_copy(j, 0).start()
        rp_copy(j, 1).start()

    for d in range(1, NE):
        meta_send(d).wait_send()
        ret_send(d).wait_send()
        r1_send(d).wait_send()
        r3_send(d).wait_send()
    for d in range(1, NZ):
        r2_send(d).wait_send()
    rc_send().wait_send()
    r4_send().wait_send()
    for e in range(n_exp):
        core_hop(TICKS - 2, e).wait_send()
        core_hop(TICKS - 1, e).wait_send()
    for v in range(2):
        for k in range(4):
            z_hop(v, k).wait_send()
        dw_copy(v).wait()
    for e in range(n_exp):
        for q in range(3):
            hg_copy(e, q).wait()
    ig_copy.wait()
    for j in range(NE):
        rp_copy(j, 0).wait()
        rp_copy(j, 1).wait()


def local(inputs, out_grad, combine, routes, saved_hidden, down_weight, router_weight):
    tokens, width = out_grad.shape
    n_exp, _, ff = down_weight.shape
    total = router_weight.shape[0]
    slots = saved_hidden.shape[2] * saved_hidden.shape[3]
    pair = slots // (NE // 2)
    hidden = saved_hidden.reshape(n_exp, slots, ff)
    dma = pltpu.SemaphoreType.DMA
    hg, dw, ig, rp = pl.pallas_call(
        fused,
        out_shape=(
            pltpu.VMEM((n_exp, slots, ff), BF),
            pltpu.VMEM((n_exp, width // NDP, ff), BF),
            pltpu.VMEM((tokens, width), BF),
            pltpu.VMEM((total, width), F32),
        ),
        in_specs=[pl.BlockSpec(memory_space=pl.ANY)] * 7,
        out_specs=(pl.BlockSpec(memory_space=pltpu.VMEM),) * 4,
        scratch_shapes=[
            pltpu.VMEM((TICKS, 2, NY, NX, tokens, LANE), BF),
            pltpu.VMEM((TICKS, n_exp, 2, LANE, ff), BF),
            pltpu.VMEM((n_exp, slots, ff), BF),
            pltpu.VMEM((n_exp, slots, ff), F32),
            pltpu.VMEM((n_exp, slots, 2 * LANE), BF),
            pltpu.VMEM((NE // 2, n_exp * pair, 2 * LANE), BF),
            pltpu.VMEM((NE // 2, n_exp * pair, LANE), F32),
            pltpu.VMEM((NE, 16, LANE), F32),
            pltpu.VMEM((8, LANE), jnp.int32),
            pltpu.VMEM((NE * n_exp, LANE), F32),
            pltpu.VMEM((NE * n_exp, LANE), F32),
            pltpu.VMEM((NE // 2, 8, 2 * LANE), F32),
            pltpu.VMEM((NE, 8, LANE), F32),
            pltpu.VMEM((NE, 8, LANE), F32),
            pltpu.VMEM((2, n_exp, LANE, ff), BF),
            pltpu.VMEM((TICKS, n_exp, LANE, ff), BF),
            pltpu.VMEM((TICKS, n_exp, LANE, ff), BF),
            pltpu.VMEM((2, 2, LANE, ff), BF),
            pltpu.VMEM((2, 2, LANE, ff), BF),
            pltpu.VMEM((2, n_exp, LANE, ff), BF),
            pltpu.VMEM((2, n_exp, LANE, ff), BF),
            pltpu.VMEM((tokens, width), BF),
            pltpu.VMEM((total, width), BF),
            pltpu.VMEM((tokens, width), BF),
            pltpu.VMEM((NE, 2, total // 2, LANE), F32),
            pltpu.VMEM((NE, total // 2, LANE), F32),
            pltpu.VMEM((NE, total // 2, LANE), F32),
            pltpu.VMEM((NZ, total // 2, LANE), F32),
            pltpu.VMEM((NE, 2, total // 2, LANE), F32),
            dma((TICKS, 2, 8)),
            dma((TICKS, 2, 8)),
            dma((TICKS, 2)),
            dma((TICKS, 2)),
            dma((5,)),
            dma((n_exp, 3)),
            dma((4,)),
            dma((NE,)),
            dma((NE,)),
            dma((NE,)),
            dma((NE,)),
            dma((TICKS, n_exp)),
            dma((TICKS, n_exp)),
            dma((2, 4)),
            dma((2, 4)),
            dma((NE,)),
            dma((NE,)),
            dma((NZ,)),
            dma((NZ,)),
            dma((NE,)),
            dma((NE,)),
            dma((2,)),
            dma((2,)),
            dma((NE, 2)),
        ],
        compiler_params=pltpu.CompilerParams(
            collective_id=0, has_side_effects=True, vmem_limit_bytes=58 * 2**20
        ),
        name="moe_down_backward",
    )(combine.T, routes.T, out_grad, hidden, down_weight, inputs, router_weight)
    return hg.reshape(saved_hidden.shape), dw, ig, rp


def solution(mesh):
    placed = (
        P(("dp", "expert"), None),
        P(("dp", "expert"), None),
        P(("dp", "expert"), None),
        P(("dp", "expert"), None),
        P("dp", "expert", None, None, None),
        P("expert", None, None),
        P(),
    )
    return jax.shard_map(
        local,
        mesh=mesh,
        in_specs=placed,
        out_specs=(
            P("dp", "expert", None, None, None),
            P("expert", "dp", None),
            P(("dp", "expert"), None),
            P(),
        ),
        check_vma=False,
    )
```
